32 devices in a mesh: tmpl: 2 (over core), row: 16 (over z, y, x).
Axes of the slice: x: 2, y: 2, z: 4, core: 2. Of those that a mesh axis runs over, the one named last changes fastest.
Arguments:
- pair_maps: bfloat16 [2, 2048, 2048, 64], P('tmpl', 'row'), may hold values from -6 to 6
- crop_tiles: int32 [2, 8], P('tmpl'), may hold values from 0 to 15, as said below
- full_length: int32 [1], replicated, may hold values from 1536 to 2048
- proj_weight: bfloat16 [2, 64, 320], replicated, may hold values from -0.75 to 0.75
- out_weight: bfloat16 [2, 64, 64], replicated, may hold values from -0.75 to 0.75
- final_weight: bfloat16 [64, 128], replicated, may hold values from -0.75 to 0.75
Outputs:
- embedding: bfloat16 [128, 1024, 1024], P(None, 'row')
The draws below stay inside these ranges and needn't reach their ends.
Inputs may be any that keep to these rules, and one draw needn't show every extreme that they name: Each row of crop_tiles names 8 different tiles of the 16, in increasing order; its last 4 entries are the tiles 16 - 8 // 2 to 15.
All inputs are finite; a program needn't handle non-finite values.
Results may differ from the reference program's by a relative error of at most 0.014.
Values may be sent and summed in bfloat16 or wider, within the bound.
A program may use at most 256 MiB of HBM per device.

```python
import jax
import jax.numpy as jnp
from jax import lax

CH = 64
CZ = 128
CROP = 1024
TILE = 128
NLAYER = 2
FULL = 2048
TEMPLATES = 2
NTILES = 16
NCROP = 8


def draw_crop_tiles(key, part):
    keys = jax.random.split(jax.random.fold_in(key, 17), TEMPLATES)
    tail_count = NCROP // 2
    head_pool = NTILES - tail_count
    tail_tiles = (jnp.arange(tail_count, dtype=jnp.int32) + head_pool).astype(jnp.int32)

    def one_template(single_key):
        order = jax.random.permutation(single_key, head_pool)
        head_tiles = jnp.sort(order[:NCROP - tail_count]).astype(jnp.int32)
        return jnp.concatenate([head_tiles, tail_tiles]).astype(jnp.int32)
    return jax.vmap(one_template)(keys)


def shard_levels(key, dims, cuts, smallest, top_value):
    gain, own = 1.0, jax.random.fold_in(key, 6)
    for dim, shards_of in cuts:
        steps = jnp.exp(jax.random.uniform(jax.random.fold_in(own, dim), (shards_of,), jnp.float32, smallest / len(cuts), top_value / len(cuts)))
        gain = gain * jnp.repeat(steps, dims[dim] // shards_of).reshape([-1 if axis == dim else 1 for axis in range(len(dims))])
    return gain


def gaussian(rng, dims, scale, bound, cuts=(), held_as=jnp.bfloat16):
    values = jax.random.normal(rng, dims, jnp.float32) * scale
    if len(cuts) > 0:
        values = shard_levels(rng, dims, cuts, -0.22, 0.18) * values
    return jnp.clip(values, min=-bound, max=bound).astype(held_as)


def setup_inputs(seed: int = 0) -> dict:
    streams_of = jax.random.split(jax.random.key(seed), 7)
    pair_maps = gaussian(streams_of[0], (TEMPLATES, FULL, FULL, CH), 1.0, 6.0, ((0, 2), (1, 16)))
    crop_tiles = draw_crop_tiles(jax.random.fold_in(streams_of[6], 71), 0)
    full_length = jax.random.randint(streams_of[2], (1,), FULL - CROP // 2, FULL + 1).astype(jnp.int32)
    proj_weight = gaussian(streams_of[3], (NLAYER, CH, 5 * CH), CH ** -0.5, 0.75)
    out_weight = gaussian(streams_of[4], (NLAYER, CH, CH), CH ** -0.5, 0.75)
    final_weight = gaussian(streams_of[5], (CH, CZ), CH ** -0.5, 0.75)
    return {"pair_maps": pair_maps, "crop_tiles": crop_tiles, "full_length": full_length, "proj_weight": proj_weight, "out_weight": out_weight, "final_weight": final_weight}


EPSILON = 1e-05

def channel_norm(values, axis_pos):
    center = values - lax.optimization_barrier(jnp.mean(values, axis=axis_pos, keepdims=True))
    spread = lax.optimization_barrier(jnp.mean(center * center, axis=axis_pos, keepdims=True))
    return center * lax.rsqrt(spread + EPSILON)

def outgoing_layer(current, usable, w_proj, w_out):
    normed_in = channel_norm(current.astype(jnp.float32), -1).astype(jnp.bfloat16)
    projected = jnp.dot(normed_in.reshape(-1, CH), w_proj, preferred_element_type=jnp.float32).reshape(CROP, CROP, 5 * CH)
    pair_mask = (usable[:, None] * usable[None, :])[:, :, None]
    left_proj = (jax.nn.sigmoid(projected[..., :CH]) * projected[..., CH:2 * CH] * pair_mask).astype(jnp.bfloat16)
    right_proj = (jax.nn.sigmoid(projected[..., 2 * CH:3 * CH]) * projected[..., 3 * CH:4 * CH] * pair_mask).astype(jnp.bfloat16)
    gate_vals = jax.nn.sigmoid(projected[..., 4 * CH:])
    left_first = jnp.transpose(left_proj, (2, 0, 1)).astype(jnp.float32)
    right_first = jnp.transpose(right_proj, (2, 0, 1)).astype(jnp.float32)
    products = jnp.einsum('cik,cjk->cij', left_first, right_first).astype(jnp.bfloat16)
    products = jnp.transpose(products, (1, 2, 0))
    normed_out = channel_norm(products.astype(jnp.float32), -1).astype(jnp.bfloat16)
    update = jnp.dot(normed_out.reshape(-1, CH), w_out, preferred_element_type=jnp.float32).reshape(CROP, CROP, CH)
    return (current.astype(jnp.float32) + gate_vals * update).astype(jnp.bfloat16)

def reference(pair_maps, crop_tiles, full_length, proj_weight, out_weight, final_weight):
    total = jnp.zeros((CROP, CROP, CH), jnp.float32)
    steps_crop = jnp.arange(CROP, dtype=jnp.int32)
    for template_idx in range(TEMPLATES):
        crop_ids = crop_tiles[template_idx].astype(jnp.int32)
        position = crop_ids[steps_crop // TILE] * TILE + steps_crop % TILE
        usable = (position < full_length[0]).astype(jnp.float32)
        full_map = pair_maps[template_idx].reshape(NTILES, TILE, FULL, CH)[crop_ids]
        full_map = full_map.reshape(CROP, NTILES, TILE, CH)[:, crop_ids]
        current = full_map.reshape(CROP, CROP, CH)
        for layer_idx in range(NLAYER):
            current = outgoing_layer(current, usable, proj_weight[layer_idx], out_weight[layer_idx])
        total = total + channel_norm(current.astype(jnp.float32), -1)
    mean_pair = total / TEMPLATES
    hidden = jnp.maximum(mean_pair, 0.0).astype(jnp.bfloat16)
    result = jnp.dot(hidden.reshape(-1, CH), final_weight, preferred_element_type=jnp.float32).reshape(CROP, CROP, CZ)
    return jnp.transpose(result, (2, 1, 0)).astype(jnp.bfloat16)
```

```python
import jax
import jax.numpy as jnp
from jax import lax
from jax.experimental import pallas as pl
from jax.experimental.pallas import tpu as pltpu
from jax.sharding import Mesh, PartitionSpec as P

CH = 64
CROP = 1024
TILE = 128
NLAYER = 2
FULL = 2048


EPSILON = 1e-05


def from_partner(value, axis, bit):
    mask = 2**bit
    pairs = [(source, source ^ mask) for source in range(lax.axis_size(axis))]
    return lax.ppermute(value, axis, pairs)


def channel_norm(values):
    center = values - jnp.mean(values, axis=0, keepdims=True)
    spread = jnp.mean(center * center, axis=0, keepdims=True)
    return center * lax.rsqrt(spread + EPSILON)


SPLIT = 2


def product_kernel(left_ref, *refs):
    rights, out_ref = refs[:-1], refs[-1]
    sources, _, width, chunk = left_ref.shape
    left = left_ref[...].reshape(sources * width, chunk)
    per = out_ref.shape[0] // len(rights)
    for number, right_ref in enumerate(rights):
        right = right_ref[...].reshape(sources * width, right_ref.shape[-1])
        product = lax.dot_general(
            right, left, (((0,), (0,)), ((), ())), preferred_element_type=jnp.float32
        )
        out_ref[number * per : (number + 1) * per] = product.astype(out_ref.dtype).reshape(
            per, 1, width, chunk
        )


def channel_products(left, rights):
    sources, channels, width, chunk = left.shape
    spec = pl.BlockSpec((sources, 1, width, chunk), lambda c: (0, c, 0, 0))
    depth = sources * width
    return pl.pallas_call(
        product_kernel,
        grid=(channels,),
        in_specs=[spec] * (1 + len(rights)),
        out_specs=spec,
        out_shape=jax.ShapeDtypeStruct(left.shape, left.dtype),
        compiler_params=pltpu.CompilerParams(vmem_limit_bytes=32 << 20),
        cost_estimate=pl.CostEstimate(
            flops=2 * channels * depth * depth * chunk,
            bytes_accessed=2 * left.size * (2 + len(rights)),
            transcendentals=0,
        ),
    )(left, *rights)


def spread_kernel(send_ref, got_ref, hold, send_sem, recv_sem, hold_sem):
    core, half, inner = (lax.axis_index(name) for name in ("core", "half", "inner"))
    cores, halves, width = (lax.axis_size(name) for name in ("core", "half", "inner"))
    blocks = cores * width
    row = half * width + inner
    mine = core * width + inner
    barrier = pltpu.get_barrier_semaphore()
    total = cores * halves * width
    flat = (core * halves + half) * width + inner
    for step in range(1, total):
        other = lax.rem(flat + step, total)
        pl.semaphore_signal(
            barrier,
            inc=1,
            device_id={
                "core": other // (halves * width),
                "half": lax.rem(other // width, halves),
                "inner": lax.rem(other, width),
            },
            device_id_type=pl.DeviceIdType.MESH,
        )
    pl.semaphore_wait(barrier, total - 1)

    def outgoing(step):
        block = lax.rem(mine + step, blocks)
        return pltpu.make_async_remote_copy(
            src_ref=send_ref.at[block],
            dst_ref=got_ref.at[row],
            send_sem=send_sem.at[step],
            recv_sem=recv_sem.at[row],
            device_id={"core": block // width, "half": core, "inner": lax.rem(block, width)},
            device_id_type=pl.DeviceIdType.MESH,
        )

    home = half == core
    for step in range(1, blocks):
        outgoing(step).start()

    @pl.when(home)
    def _():
        bring = pltpu.make_async_copy(send_ref.at[mine], hold, hold_sem.at[0])
        bring.start()
        bring.wait()
        put = pltpu.make_async_copy(hold, got_ref.at[row], hold_sem.at[1])
        put.start()
        put.wait()

    @pl.when(jnp.logical_not(home))
    def _():
        outgoing(0).start()

    def incoming(slot):
        return pltpu.make_async_remote_copy(
            src_ref=send_ref.at[0],
            dst_ref=got_ref.at[slot],
            send_sem=send_sem.at[0],
            recv_sem=recv_sem.at[slot],
            device_id={"core": core, "half": half, "inner": inner},
            device_id_type=pl.DeviceIdType.MESH,
        )

    for step in range(1, blocks):
        outgoing(step).wait_send()

    @pl.when(jnp.logical_not(home))
    def _():
        outgoing(0).wait_send()

    for step in range(1, blocks):
        incoming(lax.rem(row + step, blocks)).wait_recv()

    @pl.when(jnp.logical_not(home))
    def _():
        incoming(row).wait_recv()


def spread(send):
    blocks = send.shape[0]
    return pl.pallas_call(
        spread_kernel,
        in_specs=[pl.BlockSpec(memory_space=pl.ANY)],
        out_specs=pl.BlockSpec(memory_space=pl.ANY),
        out_shape=jax.ShapeDtypeStruct(send.shape, send.dtype),
        scratch_shapes=[
            pltpu.VMEM(send.shape[1:], send.dtype),
            pltpu.SemaphoreType.DMA((blocks,)),
            pltpu.SemaphoreType.DMA((blocks,)),
            pltpu.SemaphoreType.DMA((2,)),
        ],
        compiler_params=pltpu.CompilerParams(
            collective_id=0, has_side_effects=True, vmem_limit_bytes=32 << 20
        ),
    )(send)


GROUP = ("core", "inner")


def exchange(value):
    return lax.all_to_all(value, GROUP, split_axis=0, concat_axis=0, tiled=True)


def moved(value, pairs):
    halves = lax.axis_size("half")
    steps = [(a * halves + b, c * halves + d) for (a, b), (c, d) in pairs]
    return lax.ppermute(value, ("core", "half"), steps)


def in_halves(pair_maps, crop_tiles, full_length, proj_weight, out_weight, final_weight):
    cores, halves, inner_count = (lax.axis_size(name) for name in ("core", "half", "inner"))
    core, half, inner = (lax.axis_index(name) for name in ("core", "half", "inner"))
    row_count = cores * inner_count
    my_index = core * inner_count + inner
    col_width = CROP // row_count
    per_group = CH // row_count
    tiles = CROP // TILE
    chunk = CROP // SPLIT
    held_ids = crop_tiles[0]
    other_ids = lax.ppermute(held_ids, "core", [(0, 1), (1, 0)])
    crop_ids = jnp.where(core == half, held_ids, other_ids)
    steps_crop = jnp.arange(CROP, dtype=jnp.int32)
    position = crop_ids[steps_crop // TILE] * TILE + steps_crop % TILE
    usable = (position < full_length[0]).astype(jnp.float32)
    col_usable = lax.dynamic_slice_in_dim(usable, my_index * col_width, col_width)
    pair_mask = col_usable[:, None] * usable[None, :]
    masks = jnp.split(pair_mask, SPLIT, axis=1)
    by_channel = jnp.transpose(pair_maps[0], (0, 2, 1))
    columns = jnp.concatenate(
        [
            lax.dynamic_slice_in_dim(by_channel, held_ids[tile] * TILE, TILE, axis=2)
            for tile in range(tiles)
        ],
        axis=2,
    )
    send = jnp.transpose(columns, (2, 1, 0)).reshape(row_count, col_width, CH, TILE)
    got = spread(send)
    per = tiles // SPLIT
    current = []
    for number in range(SPLIT):
        pieces = [
            lax.dynamic_index_in_dim(got, crop_ids[number * per + tile], 0, keepdims=False)
            for tile in range(per)
        ]
        current.append(jnp.transpose(jnp.concatenate(pieces, axis=2), (1, 0, 2)))
    for layer_idx in range(NLAYER):
        lefts, rights, gates = [], [], []
        for values, mask in zip(current, masks):
            normed_in = channel_norm(values.astype(jnp.float32)).astype(jnp.bfloat16)
            projected = jnp.einsum(
                "cd,cwi->dwi", proj_weight[layer_idx], normed_in, preferred_element_type=jnp.float32
            )
            left = jax.nn.sigmoid(projected[:CH]) * projected[CH : 2 * CH] * mask
            right = jax.nn.sigmoid(projected[2 * CH : 3 * CH]) * projected[3 * CH : 4 * CH] * mask
            shape = (row_count, per_group, col_width, chunk)
            rights.append(exchange(right.astype(jnp.bfloat16).reshape(shape)))
            lefts.append(exchange(left.astype(jnp.bfloat16).reshape(shape)))
            gates.append(jax.nn.sigmoid(projected[4 * CH :]))
        following = []
        for values, left, gate in zip(current, lefts, gates):
            merged = exchange(channel_products(left, rights)).reshape(CH, col_width, chunk)
            normed_out = channel_norm(merged.astype(jnp.float32)).astype(jnp.bfloat16)
            update = jnp.einsum(
                "cd,cwi->dwi", out_weight[layer_idx], normed_out, preferred_element_type=jnp.float32
            )
            following.append((values.astype(jnp.float32) + gate * update).astype(jnp.bfloat16))
        current = following
    results = []
    for values in current:
        normed_final = channel_norm(values.astype(jnp.float32)).astype(jnp.bfloat16)
        across = moved(normed_final, [((0, 1), (0, 0)), ((1, 0), (1, 1))])
        summed = normed_final.astype(jnp.float32) + across.astype(jnp.float32)
        hidden = jnp.maximum(summed / halves, 0.0).astype(jnp.bfloat16)
        shared = moved(hidden, [((0, 0), (1, 0)), ((1, 1), (0, 1))])
        hidden = jnp.where(core == half, hidden, shared)
        results.append(
            jnp.einsum("cz,cwi->zwi", final_weight, hidden, preferred_element_type=jnp.float32)
            .astype(jnp.bfloat16)
        )
    return jnp.concatenate(results, axis=2)


def on_device(pair_maps, crop_tiles, full_length, proj_weight, out_weight, final_weight):
    row_count = lax.axis_size("row")
    my_index = lax.axis_index("row")
    pair_local = pair_maps[0]
    crop_ids = crop_tiles[0]
    local_rows = pair_local.shape[0]
    col_width = CROP // row_count
    parts_count = max(1, row_count // CH)
    per_group = CH * parts_count // row_count
    groups = CH // per_group
    part_rows = CROP // parts_count
    steps_crop = jnp.arange(CROP, dtype=jnp.int32)
    position = crop_ids[steps_crop // TILE] * TILE + steps_crop % TILE
    usable = (position < full_length[0]).astype(jnp.float32)
    col_usable = lax.dynamic_slice_in_dim(usable, my_index * col_width, col_width)
    pair_mask = col_usable[:, None] * usable[None, :]
    columns = pair_local.reshape(local_rows, FULL // TILE, TILE, CH)[:, crop_ids]
    columns = columns.reshape(local_rows, CROP * CH)
    received = lax.all_to_all(columns, "row", split_axis=1, concat_axis=0, tiled=True)
    cropped = received.reshape(FULL // TILE, TILE, col_width * CH)[crop_ids]
    current = jnp.transpose(cropped.reshape(CROP, col_width, CH), (2, 1, 0))
    for layer_idx in range(NLAYER):
        normed_in = channel_norm(current.astype(jnp.float32)).astype(jnp.bfloat16)
        projected = jnp.einsum(
            "cd,cwi->dwi", proj_weight[layer_idx], normed_in, preferred_element_type=jnp.float32
        )
        left_proj = (jax.nn.sigmoid(projected[:CH]) * projected[CH : 2 * CH] * pair_mask).astype(
            jnp.bfloat16
        )
        right_proj = (
            jax.nn.sigmoid(projected[2 * CH : 3 * CH]) * projected[3 * CH : 4 * CH] * pair_mask
        ).astype(jnp.bfloat16)
        gate_vals = jax.nn.sigmoid(projected[4 * CH :])
        left_send = left_proj.reshape(groups, per_group, col_width, parts_count, part_rows)
        left_send = jnp.transpose(left_send, (0, 3, 1, 2, 4)).reshape(
            row_count, per_group, col_width, part_rows
        )
        right_send = right_proj.reshape(groups, per_group, col_width, parts_count, part_rows)
        right_send = jnp.transpose(right_send, (0, 3, 1, 2, 4)).reshape(
            row_count, per_group, col_width, part_rows
        )
        left_got, right_got = (
            lax.all_to_all(left_send, "row", split_axis=0, concat_axis=2, tiled=True),
            lax.all_to_all(right_send, "row", split_axis=0, concat_axis=2, tiled=True),
        )
        right_whole = right_got[0]
        for bit_pos in range(parts_count.bit_length() - 1):
            partner = from_partner(right_whole, "row", bit_pos)
            lower_side = my_index // (1 << bit_pos) % 2 == 0
            right_whole = jnp.where(
                lower_side,
                jnp.concatenate([right_whole, partner], axis=2),
                jnp.concatenate([partner, right_whole], axis=2),
            )
        products = jnp.einsum(
            "cki,ckj->cij", left_got[0], right_whole, preferred_element_type=jnp.float32
        ).astype(jnp.bfloat16)
        back_send = jnp.transpose(
            products.reshape(per_group, part_rows, row_count, col_width), (2, 0, 3, 1)
        )
        back_got = lax.all_to_all(back_send, "row", split_axis=0, concat_axis=0, tiled=True)
        merged = back_got.reshape(groups, parts_count, per_group, col_width, part_rows)
        merged = jnp.transpose(merged, (0, 2, 3, 1, 4)).reshape(CH, col_width, CROP)
        normed_out = channel_norm(merged.astype(jnp.float32)).astype(jnp.bfloat16)
        update = jnp.einsum(
            "cd,cwi->dwi", out_weight[layer_idx], normed_out, preferred_element_type=jnp.float32
        )
        current = (current.astype(jnp.float32) + gate_vals * update).astype(jnp.bfloat16)
    normed_final = channel_norm(current.astype(jnp.float32))
    template_count = lax.axis_size("tmpl")
    summed = lax.psum(normed_final.astype(jnp.bfloat16), "tmpl").astype(jnp.float32)
    hidden = jnp.maximum(summed / template_count, 0.0).astype(jnp.bfloat16)
    result = jnp.einsum(
        "cz,cwi->zwi", final_weight, hidden, preferred_element_type=jnp.float32
    ).astype(jnp.bfloat16)
    return result


def solution(mesh):
    rows, templates = mesh.shape["row"], mesh.shape["tmpl"]
    whole_tiles = FULL // rows == TILE and CH % rows == 0
    if whole_tiles and templates == 2:
        grid = Mesh(
            mesh.devices.reshape(templates, templates, rows // templates),
            ("core", "half", "inner"),
        )
        lines = ("half", "inner")
        placed = (P("core", lines, None, None), P("core", None), P(), P(), P(), P())
        return jax.shard_map(
            in_halves, mesh=grid, in_specs=placed, out_specs=P(None, lines, None), check_vma=False
        )
    placed = (P("tmpl", "row", None, None), P("tmpl", None), P(), P(), P(), P())
    return jax.shard_map(
        on_device, mesh=mesh, in_specs=placed, out_specs=P(None, "row", None), check_vma=False
    )
```

```python
import functools

import jax
import jax.numpy as jnp
from jax import lax
from jax.experimental import pallas as pl
from jax.experimental.pallas import tpu as pltpu
from jax.sharding import Mesh, PartitionSpec as P

CH = 64
CROP = 1024
TILE = 128
NLAYER = 2
FULL = 2048


EPSILON = 1e-05


def from_partner(value, axis, bit):
    mask = 2**bit
    pairs = [(source, source ^ mask) for source in range(lax.axis_size(axis))]
    return lax.ppermute(value, axis, pairs)


def channel_norm(values):
    center = values - jnp.mean(values, axis=0, keepdims=True)
    spread = jnp.mean(center * center, axis=0, keepdims=True)
    return center * lax.rsqrt(spread + EPSILON)


SPLIT = 2
SUB = 8
PARTS = 2


def widened(weight, source):
    depth, columns = weight.shape
    size = source.shape[0]
    pick = (source == lax.broadcasted_iota(jnp.int32, (size, columns), 1)).astype(weight.dtype)
    taken = lax.dot_general(
        pick, weight, (((1,), (1,)), ((), ())), preferred_element_type=jnp.float32
    ).astype(weight.dtype)
    grow = lax.broadcasted_iota(jnp.int32, (depth, depth * SUB), 1) // SUB
    grow = (grow == lax.broadcasted_iota(jnp.int32, grow.shape, 0)).astype(weight.dtype)
    wide = jnp.dot(taken, grow, preferred_element_type=jnp.float32)
    row = lax.broadcasted_iota(jnp.int32, wide.shape, 0) % SUB
    lane = lax.broadcasted_iota(jnp.int32, wide.shape, 1) % SUB
    return jnp.where(row == lane, wide, 0.0).astype(weight.dtype)


def widen_kernel(proj_ref, out_ref, final_ref, wide_ref, out_wide_ref, final_wide_ref):
    size = CH // PARTS
    for layer in range(NLAYER):
        for part in range(PARTS):
            rows = lax.broadcasted_iota(jnp.int32, (5 * size * SUB, 5 * CH), 0) // SUB
            source = rows // size * CH + part * size + rows % size
            wide_ref[layer, part] = widened(proj_ref[layer], source)
        rows = lax.broadcasted_iota(jnp.int32, (CH * SUB, CH), 0) // SUB
        out_wide_ref[layer] = widened(out_ref[layer], rows)
    columns = final_ref.shape[1]
    rows = lax.broadcasted_iota(jnp.int32, (columns * SUB, columns), 0) // SUB
    final_wide_ref[...] = widened(final_ref[...], rows)


def widen(proj_weight, out_weight, final_weight):
    kind = proj_weight.dtype
    return pl.pallas_call(
        widen_kernel,
        out_shape=[
            jax.ShapeDtypeStruct((NLAYER, PARTS, 5 * CH // PARTS * SUB, CH * SUB), kind),
            jax.ShapeDtypeStruct((NLAYER, CH * SUB, CH * SUB), kind),
            jax.ShapeDtypeStruct((final_weight.shape[1] * SUB, CH * SUB), kind),
        ],
        compiler_params=PARAMS,
    )(proj_weight, out_weight, final_weight)


def sigmoid(values):
    return 0.5 * jnp.tanh(0.5 * values) + 0.5


def flat_dot(weight, values):
    channels, sub, lanes = values.shape
    return jnp.dot(
        weight,
        values.reshape(channels * sub, lanes).astype(jnp.bfloat16),
        preferred_element_type=jnp.float32,
    ).reshape(weight.shape[0] // sub, sub, lanes)


def project(values, wide_ref, mask_ref, left_ref, right_ref, gate_ref):
    normed = channel_norm(values)
    mask = mask_ref[...][None]
    size = CH // PARTS
    for part in range(PARTS):
        projected = flat_dot(wide_ref[part], normed)
        piece = slice(part * size, (part + 1) * size)
        left = sigmoid(projected[:size]) * projected[size : 2 * size] * mask
        left_ref[piece] = left.astype(left_ref.dtype)
        right = sigmoid(projected[2 * size : 3 * size]) * projected[3 * size : 4 * size] * mask
        right_ref[piece] = right.astype(right_ref.dtype)
        gate_ref[piece] = sigmoid(projected[4 * size :]).astype(gate_ref.dtype)


def updated(values, back_ref, gate_ref, out_ref):
    normed = channel_norm(back_ref[...].astype(jnp.float32))
    update = flat_dot(out_ref[...], normed)
    pair = values + gate_ref[...].astype(jnp.float32) * update
    return pair.astype(jnp.bfloat16)


def tiles_of(refs):
    return jnp.concatenate([ref[...].astype(jnp.float32) for ref in refs], axis=-1)


def first_kernel(tiles, ids_ref, *refs):
    project(tiles_of(refs[:tiles]), *refs[tiles:])


def middle_kernel(tiles, ids_ref, *refs):
    back_ref, gate_ref, out_ref, wide_ref, mask_ref = refs[tiles : tiles + 5]
    pair_ref, left_ref, right_ref, next_ref = refs[tiles + 5 :]
    pair = updated(tiles_of(refs[:tiles]), back_ref, gate_ref, out_ref)
    pair_ref[...] = pair
    project(pair.astype(jnp.float32), wide_ref, mask_ref, left_ref, right_ref, next_ref)


def last_kernel(pair_ref, back_ref, gate_ref, out_ref, final_ref):
    pair = updated(pair_ref[...].astype(jnp.float32), back_ref, gate_ref, out_ref)
    final_ref[...] = channel_norm(pair.astype(jnp.float32)).astype(final_ref.dtype)


def end_kernel(home_ref, *refs):
    hiddens, shareds = refs[: len(refs) // 2 - 1], refs[len(refs) // 2 - 1 : -2]
    wide_ref, out_ref = refs[-2:]
    home = home_ref[0] == 1
    lanes = hiddens[0].shape[-1]
    for number, (hidden_ref, shared_ref) in enumerate(zip(hiddens, shareds)):
        hidden = jnp.where(
            home, hidden_ref[...].astype(jnp.float32), shared_ref[...].astype(jnp.float32)
        )
        out_ref[:, :, number * lanes : (number + 1) * lanes] = flat_dot(
            wide_ref[...], hidden
        ).astype(out_ref.dtype)


PARAMS = pltpu.CompilerParams(vmem_limit_bytes=48 << 20)


def cost(flops, moved_bytes):
    return pl.CostEstimate(flops=int(flops), bytes_accessed=int(moved_bytes), transcendentals=0)


def by_columns(shape):
    return pl.BlockSpec((shape[0], SUB, shape[2]), lambda w, *_: (0, w, 0))


def whole(shape):
    return pl.BlockSpec(shape, lambda w, *_: (0,) * len(shape))


def layer_of(shape, layer):
    return pl.BlockSpec((None, *shape[1:]), lambda w, *_: (layer,) + (0,) * (len(shape) - 1))


def tile_specs(got, number, per):
    def at(tile):
        return pl.BlockSpec(
            (None, got.shape[1], SUB, got.shape[3]),
            lambda w, ids: (ids[number * per + tile], 0, w, 0),
        )

    return [at(tile) for tile in range(per)]


def stage(kernel, specs, out_shapes, ids, operands, flops):
    moved_bytes = sum(2 * shape.size for shape in out_shapes) * 2
    width = out_shapes[0].shape[1]
    return pl.pallas_call(
        kernel,
        grid_spec=pltpu.PrefetchScalarGridSpec(
            num_scalar_prefetch=1,
            grid=(width // SUB,),
            in_specs=specs,
            out_specs=[by_columns(shape.shape) for shape in out_shapes],
        ),
        out_shape=out_shapes,
        compiler_params=PARAMS,
        cost_estimate=cost(flops, moved_bytes),
    )(ids, *operands)


def first_stage(number, per, ids, got, wide, mask):
    _, channels, width, tile = got.shape
    shape = jax.ShapeDtypeStruct((channels, width, per * tile), got.dtype)
    specs = tile_specs(got, number, per) + [
        layer_of(wide.shape, 0),
        pl.BlockSpec((SUB, per * tile), lambda w, *_: (w, 0)),
    ]
    kernel = functools.partial(first_kernel, per)
    flops = 2 * wide.size // NLAYER * width // SUB * per * tile
    return stage(kernel, specs, [shape] * 3, ids, [got] * per + [wide, mask], flops)


def middle_stage(layer, number, per, ids, got, back, gate, out_wide, wide, mask):
    _, channels, width, tile = got.shape
    shape = jax.ShapeDtypeStruct((channels, width, per * tile), got.dtype)
    specs = tile_specs(got, number, per) + [
        by_columns(back.shape),
        by_columns(gate.shape),
        layer_of(out_wide.shape, layer),
        layer_of(wide.shape, layer + 1),
        pl.BlockSpec((SUB, per * tile), lambda w, *_: (w, 0)),
    ]
    kernel = functools.partial(middle_kernel, per)
    flops = 2 * (wide.size + out_wide.size) // NLAYER * width // SUB * per * tile
    operands = [got] * per + [back, gate, out_wide, wide, mask]
    return stage(kernel, specs, [shape] * 4, ids, operands, flops)


def last_stage(layer, pair, back, gate, out_wide):
    return pl.pallas_call(
        last_kernel,
        grid=(pair.shape[1] // SUB,),
        in_specs=[by_columns(pair.shape)] * 3 + [layer_of(out_wide.shape, layer)],
        out_specs=by_columns(pair.shape),
        out_shape=jax.ShapeDtypeStruct(pair.shape, pair.dtype),
        compiler_params=PARAMS,
        cost_estimate=cost(out_wide.size * pair.size // CH // SUB, 8 * pair.size),
    )(pair, back, gate, out_wide)


def end_stage(home, hiddens, shareds, wide):
    channels, width, lanes = hiddens[0].shape
    shape = (wide.shape[0] // SUB, width, lanes * len(hiddens))
    out = jax.ShapeDtypeStruct(shape, hiddens[0].dtype)
    specs = [by_columns(hiddens[0].shape)] * (2 * len(hiddens)) + [whole(wide.shape)]
    flops = 2 * wide.size * width // SUB * shape[2]
    return stage(end_kernel, specs, [out], home, [*hiddens, *shareds, wide], flops)[0]


def product_kernel(left_ref, *refs):
    rights, out_ref = refs[:-1], refs[-1]
    sources, _, width, chunk = left_ref.shape
    left = left_ref[...].reshape(sources * width, chunk)
    per = out_ref.shape[0] // len(rights)
    for number, right_ref in enumerate(rights):
        right = right_ref[...].reshape(sources * width, right_ref.shape[-1])
        product = lax.dot_general(
            right, left, (((0,), (0,)), ((), ())), preferred_element_type=jnp.float32
        )
        out_ref[number * per : (number + 1) * per] = product.astype(out_ref.dtype).reshape(
            per, 1, width, chunk
        )


def channel_products(left, rights):
    sources, channels, width, chunk = left.shape
    spec = pl.BlockSpec((sources, 1, width, chunk), lambda c: (0, c, 0, 0))
    depth = sources * width
    return pl.pallas_call(
        product_kernel,
        grid=(channels,),
        in_specs=[spec] * (1 + len(rights)),
        out_specs=spec,
        out_shape=jax.ShapeDtypeStruct(left.shape, left.dtype),
        compiler_params=pltpu.CompilerParams(vmem_limit_bytes=32 << 20),
        cost_estimate=pl.CostEstimate(
            flops=2 * channels * depth * depth * chunk,
            bytes_accessed=2 * left.size * (2 + len(rights)),
            transcendentals=0,
        ),
    )(left, *rights)


def spread_kernel(send_ref, got_ref, hold, send_sem, recv_sem, hold_sem):
    core, half, inner = (lax.axis_index(name) for name in ("core", "half", "inner"))
    cores, halves, width = (lax.axis_size(name) for name in ("core", "half", "inner"))
    blocks = cores * width
    row = half * width + inner
    mine = core * width + inner
    barrier = pltpu.get_barrier_semaphore()
    total = cores * halves * width
    flat = (core * halves + half) * width + inner
    for step in range(1, total):
        other = lax.rem(flat + step, total)
        pl.semaphore_signal(
            barrier,
            inc=1,
            device_id={
                "core": other // (halves * width),
                "half": lax.rem(other // width, halves),
                "inner": lax.rem(other, width),
            },
            device_id_type=pl.DeviceIdType.MESH,
        )
    pl.semaphore_wait(barrier, total - 1)

    def outgoing(step):
        block = lax.rem(mine + step, blocks)
        return pltpu.make_async_remote_copy(
            src_ref=send_ref.at[:, block],
            dst_ref=got_ref.at[row],
            send_sem=send_sem.at[step],
            recv_sem=recv_sem.at[row],
            device_id={"core": block // width, "half": core, "inner": lax.rem(block, width)},
            device_id_type=pl.DeviceIdType.MESH,
        )

    home = half == core
    for step in range(1, blocks):
        outgoing(step).start()

    @pl.when(home)
    def _():
        bring = pltpu.make_async_copy(send_ref.at[:, mine], hold, hold_sem.at[0])
        bring.start()
        bring.wait()
        put = pltpu.make_async_copy(hold, got_ref.at[row], hold_sem.at[1])
        put.start()
        put.wait()

    @pl.when(jnp.logical_not(home))
    def _():
        outgoing(0).start()

    def incoming(slot):
        return pltpu.make_async_remote_copy(
            src_ref=send_ref.at[:, 0],
            dst_ref=got_ref.at[slot],
            send_sem=send_sem.at[0],
            recv_sem=recv_sem.at[slot],
            device_id={"core": core, "half": half, "inner": inner},
            device_id_type=pl.DeviceIdType.MESH,
        )

    for step in range(1, blocks):
        outgoing(step).wait_send()

    @pl.when(jnp.logical_not(home))
    def _():
        outgoing(0).wait_send()

    for step in range(1, blocks):
        incoming(lax.rem(row + step, blocks)).wait_recv()

    @pl.when(jnp.logical_not(home))
    def _():
        incoming(row).wait_recv()


def spread(send):
    channels, blocks, width, tile = send.shape
    return pl.pallas_call(
        spread_kernel,
        in_specs=[pl.BlockSpec(memory_space=pl.ANY)],
        out_specs=pl.BlockSpec(memory_space=pl.ANY),
        out_shape=jax.ShapeDtypeStruct((blocks, channels, width, tile), send.dtype),
        scratch_shapes=[
            pltpu.VMEM((channels, width, tile), send.dtype),
            pltpu.SemaphoreType.DMA((blocks,)),
            pltpu.SemaphoreType.DMA((blocks,)),
            pltpu.SemaphoreType.DMA((2,)),
        ],
        compiler_params=pltpu.CompilerParams(
            collective_id=0, has_side_effects=True, vmem_limit_bytes=32 << 20
        ),
    )(send)


GROUP = ("core", "inner")


def exchange(value):
    return lax.all_to_all(value, GROUP, split_axis=0, concat_axis=0, tiled=True)


def moved(value, pairs):
    halves = lax.axis_size("half")
    steps = [(a * halves + b, c * halves + d) for (a, b), (c, d) in pairs]
    return lax.ppermute(value, ("core", "half"), steps)


def after(value, *others):
    return lax.optimization_barrier((value, *others))[0]


def in_halves(pair_maps, crop_tiles, full_length, proj_weight, out_weight, final_weight):
    cores, halves, inner_count = (lax.axis_size(name) for name in ("core", "half", "inner"))
    core, half, inner = (lax.axis_index(name) for name in ("core", "half", "inner"))
    row_count = cores * inner_count
    my_index = core * inner_count + inner
    col_width = CROP // row_count
    per_group = CH // row_count
    tiles = CROP // TILE
    chunk = CROP // SPLIT
    per = tiles // SPLIT
    held_ids = crop_tiles[0]
    other_ids = lax.ppermute(held_ids, "core", [(0, 1), (1, 0)])
    crop_ids = jnp.where(core == half, held_ids, other_ids)
    steps_crop = jnp.arange(CROP, dtype=jnp.int32)
    position = crop_ids[steps_crop // TILE] * TILE + steps_crop % TILE
    usable = (position < full_length[0]).astype(jnp.float32)
    col_usable = lax.dynamic_slice_in_dim(usable, my_index * col_width, col_width)
    pair_mask = col_usable[:, None] * usable[None, :]
    masks = jnp.split(pair_mask, SPLIT, axis=1)
    by_channel = jnp.transpose(pair_maps[0], (0, 2, 1))
    columns = jnp.concatenate(
        [
            lax.dynamic_slice_in_dim(by_channel, held_ids[tile] * TILE, TILE, axis=2)
            for tile in range(tiles)
        ],
        axis=2,
    )
    send = jnp.transpose(columns, (1, 2, 0)).reshape(CH, row_count, col_width, TILE)
    got = spread(send)
    wides, outs, final_wide = widen(proj_weight, out_weight, final_weight)
    shape = (row_count, per_group, col_width, chunk)
    ready = [
        first_stage(number, per, crop_ids, got, wides, masks[number]) for number in range(SPLIT)
    ]
    pairs = [None] * SPLIT
    for layer in range(NLAYER):
        lefts = [item[0].reshape(shape) for item in ready]
        rights = [exchange(item[1].reshape(shape)) for item in ready]
        gates = [item[2] for item in ready]
        following = []
        back = None
        for number in range(SPLIT):
            left = lefts[number] if back is None else after(lefts[number], back)
            back = exchange(channel_products(exchange(left), rights))
            merged = back.reshape(CH, col_width, chunk)
            if layer + 1 < NLAYER:
                pair, left, right, gate = middle_stage(
                    layer, number, per, crop_ids, got, merged, gates[number], outs, wides,
                    masks[number],
                )
                pairs[number] = pair
                following.append((left, right, gate))
            else:
                following.append(last_stage(layer, pairs[number], merged, gates[number], outs))
        ready = following
    hiddens, shareds = [], []
    for normed_final in ready:
        across = moved(normed_final, [((0, 1), (0, 0)), ((1, 0), (1, 1))])
        summed = normed_final.astype(jnp.float32) + across.astype(jnp.float32)
        hiddens.append(jnp.maximum(summed / halves, 0.0).astype(jnp.bfloat16))
        shareds.append(moved(hiddens[-1], [((0, 0), (1, 0)), ((1, 1), (0, 1))]))
    home = (core == half).astype(jnp.int32)[None]
    return end_stage(home, hiddens, shareds, final_wide)


def on_device(pair_maps, crop_tiles, full_length, proj_weight, out_weight, final_weight):
    row_count = lax.axis_size("row")
    my_index = lax.axis_index("row")
    pair_local = pair_maps[0]
    crop_ids = crop_tiles[0]
    local_rows = pair_local.shape[0]
    col_width = CROP // row_count
    parts_count = max(1, row_count // CH)
    per_group = CH * parts_count // row_count
    groups = CH // per_group
    part_rows = CROP // parts_count
    steps_crop = jnp.arange(CROP, dtype=jnp.int32)
    position = crop_ids[steps_crop // TILE] * TILE + steps_crop % TILE
    usable = (position < full_length[0]).astype(jnp.float32)
    col_usable = lax.dynamic_slice_in_dim(usable, my_index * col_width, col_width)
    pair_mask = col_usable[:, None] * usable[None, :]
    columns = pair_local.reshape(local_rows, FULL // TILE, TILE, CH)[:, crop_ids]
    columns = columns.reshape(local_rows, CROP * CH)
    received = lax.all_to_all(columns, "row", split_axis=1, concat_axis=0, tiled=True)
    cropped = received.reshape(FULL // TILE, TILE, col_width * CH)[crop_ids]
    current = jnp.transpose(cropped.reshape(CROP, col_width, CH), (2, 1, 0))
    for layer_idx in range(NLAYER):
        normed_in = channel_norm(current.astype(jnp.float32)).astype(jnp.bfloat16)
        projected = jnp.einsum(
            "cd,cwi->dwi", proj_weight[layer_idx], normed_in, preferred_element_type=jnp.float32
        )
        left_proj = (jax.nn.sigmoid(projected[:CH]) * projected[CH : 2 * CH] * pair_mask).astype(
            jnp.bfloat16
        )
        right_proj = (
            jax.nn.sigmoid(projected[2 * CH : 3 * CH]) * projected[3 * CH : 4 * CH] * pair_mask
        ).astype(jnp.bfloat16)
        gate_vals = jax.nn.sigmoid(projected[4 * CH :])
        left_send = left_proj.reshape(groups, per_group, col_width, parts_count, part_rows)
        left_send = jnp.transpose(left_send, (0, 3, 1, 2, 4)).reshape(
            row_count, per_group, col_width, part_rows
        )
        right_send = right_proj.reshape(groups, per_group, col_width, parts_count, part_rows)
        right_send = jnp.transpose(right_send, (0, 3, 1, 2, 4)).reshape(
            row_count, per_group, col_width, part_rows
        )
        left_got, right_got = (
            lax.all_to_all(left_send, "row", split_axis=0, concat_axis=2, tiled=True),
            lax.all_to_all(right_send, "row", split_axis=0, concat_axis=2, tiled=True),
        )
        right_whole = right_got[0]
        for bit_pos in range(parts_count.bit_length() - 1):
            partner = from_partner(right_whole, "row", bit_pos)
            lower_side = my_index // (1 << bit_pos) % 2 == 0
            right_whole = jnp.where(
                lower_side,
                jnp.concatenate([right_whole, partner], axis=2),
                jnp.concatenate([partner, right_whole], axis=2),
            )
        products = jnp.einsum(
            "cki,ckj->cij", left_got[0], right_whole, preferred_element_type=jnp.float32
        ).astype(jnp.bfloat16)
        back_send = jnp.transpose(
            products.reshape(per_group, part_rows, row_count, col_width), (2, 0, 3, 1)
        )
        back_got = lax.all_to_all(back_send, "row", split_axis=0, concat_axis=0, tiled=True)
        merged = back_got.reshape(groups, parts_count, per_group, col_width, part_rows)
        merged = jnp.transpose(merged, (0, 2, 3, 1, 4)).reshape(CH, col_width, CROP)
        normed_out = channel_norm(merged.astype(jnp.float32)).astype(jnp.bfloat16)
        update = jnp.einsum(
            "cd,cwi->dwi", out_weight[layer_idx], normed_out, preferred_element_type=jnp.float32
        )
        current = (current.astype(jnp.float32) + gate_vals * update).astype(jnp.bfloat16)
    normed_final = channel_norm(current.astype(jnp.float32))
    template_count = lax.axis_size("tmpl")
    summed = lax.psum(normed_final.astype(jnp.bfloat16), "tmpl").astype(jnp.float32)
    hidden = jnp.maximum(summed / template_count, 0.0).astype(jnp.bfloat16)
    result = jnp.einsum(
        "cz,cwi->zwi", final_weight, hidden, preferred_element_type=jnp.float32
    ).astype(jnp.bfloat16)
    return result


def solution(mesh):
    rows, templates = mesh.shape["row"], mesh.shape["tmpl"]
    whole_tiles = FULL // rows == TILE and CH % rows == 0
    if whole_tiles and templates == 2:
        grid = Mesh(
            mesh.devices.reshape(templates, templates, rows // templates),
            ("core", "half", "inner"),
        )
        lines = ("half", "inner")
        placed = (P("core", lines, None, None), P("core", None), P(), P(), P(), P())
        return jax.shard_map(
            in_halves, mesh=grid, in_specs=placed, out_specs=P(None, lines, None), check_vma=False
        )
    placed = (P("tmpl", "row", None, None), P("tmpl", None), P(), P(), P(), P())
    return jax.shard_map(
        on_device, mesh=mesh, in_specs=placed, out_specs=P(None, "row", None), check_vma=False
    )
```

```python
import functools

import jax
import jax.numpy as jnp
from jax import lax
from jax.experimental import pallas as pl
from jax.experimental.pallas import tpu as pltpu
from jax.sharding import Mesh, PartitionSpec as P

CH = 64
CROP = 1024
TILE = 128
NLAYER = 2
FULL = 2048


EPSILON = 1e-05


def from_partner(value, axis, bit):
    mask = 2**bit
    pairs = [(source, source ^ mask) for source in range(lax.axis_size(axis))]
    return lax.ppermute(value, axis, pairs)


def channel_norm(values):
    center = values - jnp.mean(values, axis=0, keepdims=True)
    spread = jnp.mean(center * center, axis=0, keepdims=True)
    return center * lax.rsqrt(spread + EPSILON)


SPLIT = 2
SUB = 8
PARTS = 2
COLUMN_PARTS = 2
LEFT_PARTS = 1


def widened(weight, source):
    depth, columns = weight.shape
    size = source.shape[0]
    pick = (source == lax.broadcasted_iota(jnp.int32, (size, columns), 1)).astype(weight.dtype)
    taken = lax.dot_general(
        pick, weight, (((1,), (1,)), ((), ())), preferred_element_type=jnp.float32
    ).astype(weight.dtype)
    grow = lax.broadcasted_iota(jnp.int32, (depth, depth * SUB), 1) // SUB
    grow = (grow == lax.broadcasted_iota(jnp.int32, grow.shape, 0)).astype(weight.dtype)
    wide = jnp.dot(taken, grow, preferred_element_type=jnp.float32)
    row = lax.broadcasted_iota(jnp.int32, wide.shape, 0) % SUB
    lane = lax.broadcasted_iota(jnp.int32, wide.shape, 1) % SUB
    return jnp.where(row == lane, wide, 0.0).astype(weight.dtype)


def widen_kernel(proj_ref, out_ref, final_ref, wide_ref, out_wide_ref, final_wide_ref):
    size = CH // PARTS
    for layer in range(NLAYER):
        for part in range(PARTS):
            rows = lax.broadcasted_iota(jnp.int32, (5 * size * SUB, 5 * CH), 0) // SUB
            source = rows // size * CH + part * size + rows % size
            wide_ref[layer, part] = widened(proj_ref[layer], source)
        rows = lax.broadcasted_iota(jnp.int32, (CH * SUB, CH), 0) // SUB
        out_wide_ref[layer] = widened(out_ref[layer], rows)
    columns = final_ref.shape[1]
    rows = lax.broadcasted_iota(jnp.int32, (columns * SUB, columns), 0) // SUB
    final_wide_ref[...] = widened(final_ref[...], rows)


def widen(proj_weight, out_weight, final_weight):
    kind = proj_weight.dtype
    return pl.pallas_call(
        widen_kernel,
        out_shape=[
            jax.ShapeDtypeStruct((NLAYER, PARTS, 5 * CH // PARTS * SUB, CH * SUB), kind),
            jax.ShapeDtypeStruct((NLAYER, CH * SUB, CH * SUB), kind),
            jax.ShapeDtypeStruct((final_weight.shape[1] * SUB, CH * SUB), kind),
        ],
        compiler_params=PARAMS,
    )(proj_weight, out_weight, final_weight)


def sigmoid(values):
    return 0.5 * jnp.tanh(0.5 * values) + 0.5


def flat_dot(weight, values):
    channels, sub, lanes = values.shape
    return jnp.dot(
        weight,
        values.reshape(channels * sub, lanes).astype(jnp.bfloat16),
        preferred_element_type=jnp.float32,
    ).reshape(weight.shape[0] // sub, sub, lanes)


def project(values, wide_ref, mask_ref, store):
    normed = channel_norm(values)
    mask = mask_ref[...][None]
    size = CH // PARTS
    for part in range(PARTS):
        projected = flat_dot(wide_ref[part], normed)
        left = sigmoid(projected[:size]) * projected[size : 2 * size] * mask
        right = sigmoid(projected[2 * size : 3 * size]) * projected[3 * size : 4 * size] * mask
        gate = sigmoid(projected[4 * size :])
        pieces = [item.astype(jnp.bfloat16) for item in (left, right, gate)]
        store(slice(part * size, (part + 1) * size), *pieces)


def updated(values, back_ref, gate, out_ref):
    normed = channel_norm(back_ref[...].astype(jnp.float32))
    update = flat_dot(out_ref[...], normed)
    return (values + gate * update).astype(jnp.bfloat16)


def tiles_of(refs):
    return jnp.concatenate([ref[...].astype(jnp.float32) for ref in refs], axis=-1)


def first_kernel(per, ids_ref, *refs):
    wide_ref, mask_ref, both_ref, gate_ref = refs[per:]
    _, _, group, sub, lanes = both_ref.shape

    def store(piece, left, right, gate):
        place = slice(piece.start // group, piece.stop // group)
        both_ref[place, 0] = left.reshape(-1, group, sub, lanes)
        both_ref[place, 1] = right.reshape(-1, group, sub, lanes)
        gate_ref[piece] = gate

    project(tiles_of(refs[:per]), wide_ref, mask_ref, store)


def middle_kernel(parts, per, count, ids_ref, *refs):
    tiles, refs = refs[: parts * per], refs[parts * per :]
    gates, refs = refs[:parts], refs[parts:]
    back_ref, out_ref, wide_ref, mask_ref, pair_ref, right_ref, next_ref = refs[:7]
    left_refs = refs[7:]

    def store(piece, left, right, gate):
        right_ref[piece] = right
        next_ref[piece] = gate
        for number, left_ref in enumerate(left_refs):
            lanes = left_ref.shape[-1]
            left_ref[piece] = left[:, :, number * lanes : (number + 1) * lanes]

    values = tiles_of(tiles[:per])
    gate = gates[0][...].astype(jnp.float32)
    for part in range(1, parts):
        reached = pl.program_id(0) >= part * count
        values = jnp.where(reached, tiles_of(tiles[part * per : (part + 1) * per]), values)
        gate = jnp.where(reached, gates[part][...].astype(jnp.float32), gate)
    pair = updated(values, back_ref, gate, out_ref)
    pair_ref[...] = pair
    project(pair.astype(jnp.float32), wide_ref, mask_ref, store)


def last_kernel(pair_ref, back_ref, gate_ref, out_ref, final_ref):
    gate = gate_ref[...].astype(jnp.float32)
    pair = updated(pair_ref[...].astype(jnp.float32), back_ref, gate, out_ref)
    final_ref[...] = channel_norm(pair.astype(jnp.float32)).astype(final_ref.dtype)


def end_kernel(home_ref, *refs):
    hiddens, shareds = refs[: len(refs) // 2 - 1], refs[len(refs) // 2 - 1 : -2]
    wide_ref, out_ref = refs[-2:]
    home = home_ref[0] == 1
    lanes = hiddens[0].shape[-1]
    for number, (hidden_ref, shared_ref) in enumerate(zip(hiddens, shareds)):
        hidden = jnp.where(
            home, hidden_ref[...].astype(jnp.float32), shared_ref[...].astype(jnp.float32)
        )
        out_ref[:, :, number * lanes : (number + 1) * lanes] = flat_dot(
            wide_ref[...], hidden
        ).astype(out_ref.dtype)


PARAMS = pltpu.CompilerParams(vmem_limit_bytes=48 << 20)


def cost(flops, moved_bytes):
    return pl.CostEstimate(flops=int(flops), bytes_accessed=int(moved_bytes), transcendentals=0)


def by_columns(shape):
    return pl.BlockSpec((shape[0], SUB, shape[2]), lambda w, *_: (0, w, 0))


def whole(shape):
    return pl.BlockSpec(shape, lambda w, *_: (0,) * len(shape))


def layer_of(shape, layer):
    return pl.BlockSpec((None, *shape[1:]), lambda w, *_: (layer,) + (0,) * (len(shape) - 1))


def tile_specs(got, per, place):
    def at(tile):
        def index(*position):
            number, column = place(*position[:-1])
            return position[-1][number * per + tile], 0, column, 0

        return pl.BlockSpec((None, got.shape[1], SUB, got.shape[3]), index)

    return [at(tile) for tile in range(per)]


def part_column(part, count):
    return lambda w: jnp.clip(w - part * count, 0, count - 1)


def stage(kernel, specs, out_shapes, ids, operands, flops):
    moved_bytes = sum(2 * shape.size for shape in out_shapes) * 2
    width = out_shapes[0].shape[1]
    return pl.pallas_call(
        kernel,
        grid_spec=pltpu.PrefetchScalarGridSpec(
            num_scalar_prefetch=1,
            grid=(width // SUB,),
            in_specs=specs,
            out_specs=[by_columns(shape.shape) for shape in out_shapes],
        ),
        out_shape=out_shapes,
        compiler_params=PARAMS,
        cost_estimate=cost(flops, moved_bytes),
    )(ids, *operands)


def first_stage(part, ids, got, wide, mask):
    targets, channels, width, tile = got.shape
    per = ids.shape[0] // SPLIT
    lanes = per * tile
    count = width // SUB
    group = channels // targets
    specs = tile_specs(got, per, lambda n, w: (n, w)) + [
        pl.BlockSpec((None, *wide.shape[1:]), lambda n, w, _: (0, 0, 0, 0)),
        pl.BlockSpec((SUB, lanes), lambda n, w, _: (part * count + w, n)),
    ]
    return pl.pallas_call(
        functools.partial(first_kernel, per),
        grid_spec=pltpu.PrefetchScalarGridSpec(
            num_scalar_prefetch=1,
            grid=(SPLIT, count),
            in_specs=specs,
            out_specs=[
                pl.BlockSpec((targets, 2, group, SUB, lanes), lambda n, w, _: (0, 0, 0, w, n)),
                pl.BlockSpec((channels, SUB, lanes), lambda n, w, _: (0, w, n)),
            ],
        ),
        out_shape=[
            jax.ShapeDtypeStruct((targets, 2, group, width, SPLIT * lanes), got.dtype),
            jax.ShapeDtypeStruct((channels, width, SPLIT * lanes), got.dtype),
        ],
        compiler_params=PARAMS,
        cost_estimate=cost(
            2 * wide.size // NLAYER * count * SPLIT * lanes, 8 * channels * width * SPLIT * lanes
        ),
    )(ids, *[got] * per, wide, mask)


def middle_stage(layer, number, ids, gots, back, gates, out_wide, wide, mask):
    _, channels, width, tile = gots[0].shape
    per = ids.shape[0] // SPLIT
    lanes = per * tile
    count = width // SUB
    shape = jax.ShapeDtypeStruct((channels, width * len(gots), lanes), back.dtype)
    specs, operands = [], []
    for part, got in enumerate(gots):
        column = part_column(part, count)
        specs += tile_specs(got, per, lambda w, column=column: (number, column(w)))
        operands += [got] * per
    for part, gate in enumerate(gates):
        column = part_column(part, count)
        specs.append(
            pl.BlockSpec(
                (channels, SUB, lanes), lambda w, _, column=column: (0, column(w), number)
            )
        )
        operands.append(gate)
    specs += [
        by_columns(back.shape),
        layer_of(out_wide.shape, layer),
        layer_of(wide.shape, layer + 1),
        pl.BlockSpec((SUB, lanes), lambda w, _: (w, number)),
    ]
    operands += [back, out_wide, wide, mask]
    kernel = functools.partial(middle_kernel, len(gots), per, count)
    flops = 2 * (wide.size + out_wide.size) // NLAYER * count * len(gots) * lanes
    left = jax.ShapeDtypeStruct((*shape.shape[:2], lanes // LEFT_PARTS), back.dtype)
    return stage(kernel, specs, [shape] * 3 + [left] * LEFT_PARTS, ids, operands, flops)


def last_stage(layer, piece, pair, back, gate, out_wide):
    block = pl.BlockSpec((back.shape[0], SUB, back.shape[2]), lambda w: (0, w, piece))
    return pl.pallas_call(
        last_kernel,
        grid=(back.shape[1] // SUB,),
        in_specs=[block, by_columns(back.shape), block, layer_of(out_wide.shape, layer)],
        out_specs=by_columns(back.shape),
        out_shape=jax.ShapeDtypeStruct(back.shape, back.dtype),
        compiler_params=PARAMS,
        cost_estimate=cost(out_wide.size * back.size // CH // SUB, 8 * back.size),
    )(pair, back, gate, out_wide)


def end_stage(home, hiddens, shareds, wide):
    _, width, lanes = hiddens[0].shape
    shape = (wide.shape[0] // SUB, width, lanes * len(hiddens))
    out = jax.ShapeDtypeStruct(shape, hiddens[0].dtype)
    specs = [by_columns(hiddens[0].shape)] * (2 * len(hiddens)) + [whole(wide.shape)]
    flops = 2 * wide.size * width // SUB * shape[2]
    return stage(end_kernel, specs, [out], home, [*hiddens, *shareds, wide], flops)[0]


def product_kernel(axis, count, *refs):
    lefts, rights, out_ref = refs[:count], refs[count:-1], refs[-1]
    targets, _, width, chunk = out_ref.shape

    def matrix(ref):
        value = ref[...]
        return value.reshape(value.shape[0] * value.shape[-2], value.shape[-1])

    def times(left, right):
        return lax.dot_general(
            right, left, (((0,), (0,)), ((), ())), preferred_element_type=jnp.float32
        )

    if axis == "depth":
        left = jnp.concatenate([matrix(ref) for ref in lefts], axis=0)
        right = jnp.concatenate([matrix(ref) for ref in rights], axis=0)
        pieces = [times(left, right)]
    else:
        pieces = [times(matrix(lefts[0]), matrix(right)) for right in rights]
    per = targets // len(pieces)
    for number, piece in enumerate(pieces):
        out_ref[number * per : (number + 1) * per] = piece.astype(out_ref.dtype).reshape(
            per, 1, width, chunk
        )


def product_call(axis, specs, operands, count, out):
    targets, channels, width, chunk = out.shape
    return pl.pallas_call(
        functools.partial(product_kernel, axis, count),
        grid=(channels,),
        in_specs=specs,
        out_specs=pl.BlockSpec((targets, 1, width, chunk), lambda c: (0, c, 0, 0)),
        out_shape=out,
        compiler_params=pltpu.CompilerParams(vmem_limit_bytes=40 << 20),
        cost_estimate=cost(2 * out.size * targets * width, 8 * out.size),
    )(*operands)


def depth_products(number, boths, chunk):
    targets, _, channels, width, lanes = boths[0].shape

    def spec(side, size, place):
        return pl.BlockSpec((targets, None, 1, width, size), lambda c: (0, side, c, 0, place))

    out = jax.ShapeDtypeStruct((targets, channels, width * len(boths), chunk), boths[0].dtype)
    specs = [spec(0, chunk, number)] * len(boths) + [spec(1, lanes, 0)] * len(boths)
    return product_call("depth", specs, boths + boths, len(boths), out)


def row_products(left, rights):
    targets, _, width, _ = left.shape

    def spec(array):
        return pl.BlockSpec((targets, 1, width, array.shape[3]), lambda c: (0, c, 0, 0))

    out = jax.ShapeDtypeStruct(left.shape, left.dtype)
    specs = [spec(array) for array in (left, *rights)]
    return product_call("rows", specs, [left, *rights], 1, out)


def pack_kernel(ids_ref, rows_ref, packed_ref):
    rows = rows_ref[...].astype(jnp.float32)
    packed_ref[...] = jnp.swapaxes(jnp.swapaxes(rows, 0, 1), 1, 2).astype(packed_ref.dtype)


def pack(ids, rows):
    tile, channels, _ = rows.shape
    slots = ids.shape[0]
    group = 2 * SUB
    out = jax.ShapeDtypeStruct((channels, slots * TILE, tile), rows.dtype)
    return pl.pallas_call(
        pack_kernel,
        grid_spec=pltpu.PrefetchScalarGridSpec(
            num_scalar_prefetch=1,
            grid=(slots, channels // group),
            in_specs=[pl.BlockSpec((tile, group, TILE), lambda s, c, ids: (0, c, ids[s]))],
            out_specs=pl.BlockSpec((group, TILE, tile), lambda s, c, ids: (c, s, 0)),
        ),
        out_shape=out,
        compiler_params=PARAMS,
        cost_estimate=cost(0, 4 * out.size),
    )(ids, rows)


def spread_kernel(part, send_ref, got_ref, hold, send_sem, recv_sem, hold_sem):
    columns = pl.ds(part * got_ref.shape[2], got_ref.shape[2])
    core, half, inner = (lax.axis_index(name) for name in ("core", "half", "inner"))
    cores, halves, width = (lax.axis_size(name) for name in ("core", "half", "inner"))
    blocks = cores * width
    row = half * width + inner
    mine = core * width + inner
    barrier = pltpu.get_barrier_semaphore()
    total = cores * halves * width
    flat = (core * halves + half) * width + inner
    for step in range(1, total):
        other = lax.rem(flat + step, total)
        pl.semaphore_signal(
            barrier,
            inc=1,
            device_id={
                "core": other // (halves * width),
                "half": lax.rem(other // width, halves),
                "inner": lax.rem(other, width),
            },
            device_id_type=pl.DeviceIdType.MESH,
        )
    pl.semaphore_wait(barrier, total - 1)

    def outgoing(step):
        block = lax.rem(mine + step, blocks)
        return pltpu.make_async_remote_copy(
            src_ref=send_ref.at[:, block, columns],
            dst_ref=got_ref.at[row],
            send_sem=send_sem.at[step],
            recv_sem=recv_sem.at[row],
            device_id={"core": block // width, "half": core, "inner": lax.rem(block, width)},
            device_id_type=pl.DeviceIdType.MESH,
        )

    home = half == core
    for step in range(1, blocks):
        outgoing(step).start()

    @pl.when(home)
    def _():
        bring = pltpu.make_async_copy(send_ref.at[:, mine, columns], hold, hold_sem.at[0])
        bring.start()
        bring.wait()
        put = pltpu.make_async_copy(hold, got_ref.at[row], hold_sem.at[1])
        put.start()
        put.wait()

    @pl.when(jnp.logical_not(home))
    def _():
        outgoing(0).start()

    def incoming(slot):
        return pltpu.make_async_remote_copy(
            src_ref=send_ref.at[:, 0, columns],
            dst_ref=got_ref.at[slot],
            send_sem=send_sem.at[0],
            recv_sem=recv_sem.at[slot],
            device_id={"core": core, "half": half, "inner": inner},
            device_id_type=pl.DeviceIdType.MESH,
        )

    for step in range(1, blocks):
        outgoing(step).wait_send()

    @pl.when(jnp.logical_not(home))
    def _():
        outgoing(0).wait_send()

    for step in range(1, blocks):
        incoming(lax.rem(row + step, blocks)).wait_recv()

    @pl.when(jnp.logical_not(home))
    def _():
        incoming(row).wait_recv()


def spread(send, part):
    channels, blocks, width, tile = send.shape
    width = width // COLUMN_PARTS
    return pl.pallas_call(
        functools.partial(spread_kernel, part),
        in_specs=[pl.BlockSpec(memory_space=pl.ANY)],
        out_specs=pl.BlockSpec(memory_space=pl.ANY),
        out_shape=jax.ShapeDtypeStruct((blocks, channels, width, tile), send.dtype),
        scratch_shapes=[
            pltpu.VMEM((channels, width, tile), send.dtype),
            pltpu.SemaphoreType.DMA((blocks,)),
            pltpu.SemaphoreType.DMA((blocks,)),
            pltpu.SemaphoreType.DMA((2,)),
        ],
        compiler_params=pltpu.CompilerParams(
            collective_id=part, has_side_effects=True, vmem_limit_bytes=32 << 20
        ),
        cost_estimate=cost(0, 64 * blocks * channels * width * tile),
    )(send)


GROUP = ("core", "inner")


def exchange(value):
    return lax.all_to_all(value, GROUP, split_axis=0, concat_axis=0, tiled=True)


def moved(value, pairs):
    halves = lax.axis_size("half")
    steps = [(a * halves + b, c * halves + d) for (a, b), (c, d) in pairs]
    return lax.ppermute(value, ("core", "half"), steps)


def after(value, *others):
    return lax.optimization_barrier((value, *others))[0]


def in_halves(pair_maps, crop_tiles, full_length, proj_weight, out_weight, final_weight):
    cores, halves, inner_count = (lax.axis_size(name) for name in ("core", "half", "inner"))
    core, half, inner = (lax.axis_index(name) for name in ("core", "half", "inner"))
    row_count = cores * inner_count
    my_index = core * inner_count + inner
    col_width = CROP // row_count
    per_group = CH // row_count
    chunk = CROP // SPLIT
    held_ids = crop_tiles[0]
    other_ids = lax.ppermute(held_ids, "core", [(0, 1), (1, 0)])
    crop_ids = jnp.where(core == half, held_ids, other_ids)
    steps_crop = jnp.arange(CROP, dtype=jnp.int32)
    position = crop_ids[steps_crop // TILE] * TILE + steps_crop % TILE
    usable = (position < full_length[0]).astype(jnp.float32)
    col_usable = lax.dynamic_slice_in_dim(usable, my_index * col_width, col_width)
    pair_mask = col_usable[:, None] * usable[None, :]
    send = pack(held_ids, jnp.transpose(pair_maps[0], (0, 2, 1)))
    send = send.reshape(CH, row_count, col_width, TILE)
    wides, outs, final_wide = widen(proj_weight, out_weight, final_weight)
    gots, gates, boths = [], [], []
    for part in range(COLUMN_PARTS):
        got = spread(send, part)
        both, gate = first_stage(part, crop_ids, got, wides, pair_mask)
        send = after(send, both)
        gots.append(got)
        gates.append(gate)
        boths.append(exchange(both))
    following = []
    for number in range(SPLIT):
        merged = exchange(depth_products(number, boths, chunk)).reshape(CH, col_width, chunk)
        following.append(
            middle_stage(0, number, crop_ids, gots, merged, gates, outs, wides, pair_mask)
        )
    rights = [
        exchange(item[1].reshape(row_count, per_group, col_width, chunk)) for item in following
    ]
    ready, arrived = [], []
    back = None
    for pair, _, gate, *lefts in following:
        for piece, left in enumerate(lefts):
            left = left.reshape(row_count, per_group, col_width, chunk // LEFT_PARTS)
            left = exchange(left if back is None else after(left, back, ready[-1]))
            back = exchange(row_products(left, rights))
            merged = back.reshape(CH, col_width, chunk // LEFT_PARTS)
            ready.append(last_stage(NLAYER - 1, piece, pair, merged, gate, outs))
            arrived.append(moved(ready[-1], [((0, 1), (0, 0)), ((1, 0), (1, 1))]))
    hiddens, shareds = [], []
    for normed_final, across in zip(ready, arrived):
        summed = normed_final.astype(jnp.float32) + across.astype(jnp.float32)
        hiddens.append(jnp.maximum(summed / halves, 0.0).astype(jnp.bfloat16))
        shareds.append(moved(hiddens[-1], [((0, 0), (1, 0)), ((1, 1), (0, 1))]))
    home = (core == half).astype(jnp.int32)[None]
    return end_stage(home, hiddens, shareds, final_wide)


def on_device(pair_maps, crop_tiles, full_length, proj_weight, out_weight, final_weight):
    row_count = lax.axis_size("row")
    my_index = lax.axis_index("row")
    pair_local = pair_maps[0]
    crop_ids = crop_tiles[0]
    local_rows = pair_local.shape[0]
    col_width = CROP // row_count
    parts_count = max(1, row_count // CH)
    per_group = CH * parts_count // row_count
    groups = CH // per_group
    part_rows = CROP // parts_count
    steps_crop = jnp.arange(CROP, dtype=jnp.int32)
    position = crop_ids[steps_crop // TILE] * TILE + steps_crop % TILE
    usable = (position < full_length[0]).astype(jnp.float32)
    col_usable = lax.dynamic_slice_in_dim(usable, my_index * col_width, col_width)
    pair_mask = col_usable[:, None] * usable[None, :]
    columns = pair_local.reshape(local_rows, FULL // TILE, TILE, CH)[:, crop_ids]
    columns = columns.reshape(local_rows, CROP * CH)
    received = lax.all_to_all(columns, "row", split_axis=1, concat_axis=0, tiled=True)
    cropped = received.reshape(FULL // TILE, TILE, col_width * CH)[crop_ids]
    current = jnp.transpose(cropped.reshape(CROP, col_width, CH), (2, 1, 0))
    for layer_idx in range(NLAYER):
        normed_in = channel_norm(current.astype(jnp.float32)).astype(jnp.bfloat16)
        projected = jnp.einsum(
            "cd,cwi->dwi", proj_weight[layer_idx], normed_in, preferred_element_type=jnp.float32
        )
        left_proj = (jax.nn.sigmoid(projected[:CH]) * projected[CH : 2 * CH] * pair_mask).astype(
            jnp.bfloat16
        )
        right_proj = (
            jax.nn.sigmoid(projected[2 * CH : 3 * CH]) * projected[3 * CH : 4 * CH] * pair_mask
        ).astype(jnp.bfloat16)
        gate_vals = jax.nn.sigmoid(projected[4 * CH :])
        left_send = left_proj.reshape(groups, per_group, col_width, parts_count, part_rows)
        left_send = jnp.transpose(left_send, (0, 3, 1, 2, 4)).reshape(
            row_count, per_group, col_width, part_rows
        )
        right_send = right_proj.reshape(groups, per_group, col_width, parts_count, part_rows)
        right_send = jnp.transpose(right_send, (0, 3, 1, 2, 4)).reshape(
            row_count, per_group, col_width, part_rows
        )
        left_got, right_got = (
            lax.all_to_all(left_send, "row", split_axis=0, concat_axis=2, tiled=True),
            lax.all_to_all(right_send, "row", split_axis=0, concat_axis=2, tiled=True),
        )
        right_whole = right_got[0]
        for bit_pos in range(parts_count.bit_length() - 1):
            partner = from_partner(right_whole, "row", bit_pos)
            lower_side = my_index // (1 << bit_pos) % 2 == 0
            right_whole = jnp.where(
                lower_side,
                jnp.concatenate([right_whole, partner], axis=2),
                jnp.concatenate([partner, right_whole], axis=2),
            )
        products = jnp.einsum(
            "cki,ckj->cij", left_got[0], right_whole, preferred_element_type=jnp.float32
        ).astype(jnp.bfloat16)
        back_send = jnp.transpose(
            products.reshape(per_group, part_rows, row_count, col_width), (2, 0, 3, 1)
        )
        back_got = lax.all_to_all(back_send, "row", split_axis=0, concat_axis=0, tiled=True)
        merged = back_got.reshape(groups, parts_count, per_group, col_width, part_rows)
        merged = jnp.transpose(merged, (0, 2, 3, 1, 4)).reshape(CH, col_width, CROP)
        normed_out = channel_norm(merged.astype(jnp.float32)).astype(jnp.bfloat16)
        update = jnp.einsum(
            "cd,cwi->dwi", out_weight[layer_idx], normed_out, preferred_element_type=jnp.float32
        )
        current = (current.astype(jnp.float32) + gate_vals * update).astype(jnp.bfloat16)
    normed_final = channel_norm(current.astype(jnp.float32))
    template_count = lax.axis_size("tmpl")
    summed = lax.psum(normed_final.astype(jnp.bfloat16), "tmpl").astype(jnp.float32)
    hidden = jnp.maximum(summed / template_count, 0.0).astype(jnp.bfloat16)
    result = jnp.einsum(
        "cz,cwi->zwi", final_weight, hidden, preferred_element_type=jnp.float32
    ).astype(jnp.bfloat16)
    return result


def solution(mesh):
    rows, templates = mesh.shape["row"], mesh.shape["tmpl"]
    whole_tiles = FULL // rows == TILE and CH % rows == 0
    if whole_tiles and templates == 2:
        grid = Mesh(
            mesh.devices.reshape(templates, templates, rows // templates),
            ("core", "half", "inner"),
        )
        lines = ("half", "inner")
        placed = (P("core", lines, None, None), P("core", None), P(), P(), P(), P())
        return jax.shard_map(
            in_halves, mesh=grid, in_specs=placed, out_specs=P(None, lines, None), check_vma=False
        )
    placed = (P("tmpl", "row", None, None), P("tmpl", None), P(), P(), P(), P())
    return jax.shard_map(
        on_device, mesh=mesh, in_specs=placed, out_specs=P(None, "row", None), check_vma=False
    )
```

```python
import functools

import jax
import jax.numpy as jnp
from jax import lax
from jax.experimental import pallas as pl
from jax.experimental.pallas import tpu as pltpu
from jax.sharding import Mesh, PartitionSpec as P

CH = 64
CROP = 1024
TILE = 128
NLAYER = 2
FULL = 2048


EPSILON = 1e-05


def from_partner(value, axis, bit):
    mask = 2**bit
    pairs = [(source, source ^ mask) for source in range(lax.axis_size(axis))]
    return lax.ppermute(value, axis, pairs)


def channel_norm(values):
    center = values - jnp.mean(values, axis=0, keepdims=True)
    spread = jnp.mean(center * center, axis=0, keepdims=True)
    return center * lax.rsqrt(spread + EPSILON)


SPLIT = 2
SUB = 8
PARTS = 2
COLUMN_PARTS = 2
LEFT_PARTS = 1


def widened(weight, source):
    depth, columns = weight.shape
    size = source.shape[0]
    pick = (source == lax.broadcasted_iota(jnp.int32, (size, columns), 1)).astype(weight.dtype)
    taken = lax.dot_general(
        pick, weight, (((1,), (1,)), ((), ())), preferred_element_type=jnp.float32
    ).astype(weight.dtype)
    grow = lax.broadcasted_iota(jnp.int32, (depth, depth * SUB), 1) // SUB
    grow = (grow == lax.broadcasted_iota(jnp.int32, grow.shape, 0)).astype(weight.dtype)
    wide = jnp.dot(taken, grow, preferred_element_type=jnp.float32)
    row = lax.broadcasted_iota(jnp.int32, wide.shape, 0) % SUB
    lane = lax.broadcasted_iota(jnp.int32, wide.shape, 1) % SUB
    return jnp.where(row == lane, wide, 0.0).astype(weight.dtype)


def widen_kernel(proj_ref, out_ref, final_ref, wide_ref, out_wide_ref, final_wide_ref):
    size = CH // PARTS
    for layer in range(NLAYER):
        for part in range(PARTS):
            rows = lax.broadcasted_iota(jnp.int32, (5 * size * SUB, 5 * CH), 0) // SUB
            source = rows // size * CH + part * size + rows % size
            wide_ref[layer, part] = widened(proj_ref[layer], source)
        rows = lax.broadcasted_iota(jnp.int32, (CH * SUB, CH), 0) // SUB
        out_wide_ref[layer] = widened(out_ref[layer], rows)
    columns = final_ref.shape[1]
    rows = lax.broadcasted_iota(jnp.int32, (columns * SUB, columns), 0) // SUB
    final_wide_ref[...] = widened(final_ref[...], rows)


def widen(proj_weight, out_weight, final_weight):
    kind = proj_weight.dtype
    return pl.pallas_call(
        widen_kernel,
        out_shape=[
            jax.ShapeDtypeStruct((NLAYER, PARTS, 5 * CH // PARTS * SUB, CH * SUB), kind),
            jax.ShapeDtypeStruct((NLAYER, CH * SUB, CH * SUB), kind),
            jax.ShapeDtypeStruct((final_weight.shape[1] * SUB, CH * SUB), kind),
        ],
        compiler_params=PARAMS,
    )(proj_weight, out_weight, final_weight)


def sigmoid(values):
    return 0.5 * jnp.tanh(0.5 * values) + 0.5


def flat_dot(weight, values):
    channels, sub, lanes = values.shape
    return jnp.dot(
        weight,
        values.reshape(channels * sub, lanes).astype(jnp.bfloat16),
        preferred_element_type=jnp.float32,
    ).reshape(weight.shape[0] // sub, sub, lanes)


def project(values, wide_ref, mask_ref, store):
    normed = channel_norm(values)
    mask = mask_ref[...][None]
    size = CH // PARTS
    for part in range(PARTS):
        projected = flat_dot(wide_ref[part], normed)
        left = sigmoid(projected[:size]) * projected[size : 2 * size] * mask
        right = sigmoid(projected[2 * size : 3 * size]) * projected[3 * size : 4 * size] * mask
        gate = sigmoid(projected[4 * size :])
        pieces = [item.astype(jnp.bfloat16) for item in (left, right, gate)]
        store(slice(part * size, (part + 1) * size), *pieces)


def updated(values, back_ref, gate, out_ref):
    normed = channel_norm(back_ref[...].astype(jnp.float32))
    update = flat_dot(out_ref[...], normed)
    return (values + gate * update).astype(jnp.bfloat16)


def tiles_of(refs):
    return jnp.concatenate([ref[...].astype(jnp.float32) for ref in refs], axis=-1)


def first_kernel(per, ids_ref, *refs):
    wide_ref, mask_ref, gate_ref, *send_refs = refs[per:]
    group, sub, lanes = send_refs[0].shape[-3:]

    def store(piece, left, right, gate):
        place = slice(piece.start // group, piece.stop // group)
        for side, value in enumerate((left, right)):
            value = value.reshape(-1, group, sub, lanes)
            if len(send_refs) == 1:
                send_refs[0][place, side] = value
            else:
                send_refs[side][place] = value
        gate_ref[piece] = gate

    project(tiles_of(refs[:per]), wide_ref, mask_ref, store)


def middle_kernel(parts, per, count, ids_ref, *refs):
    tiles, refs = refs[: parts * per], refs[parts * per :]
    gates, refs = refs[:parts], refs[parts:]
    back_ref, out_ref, wide_ref, mask_ref, pair_ref, right_ref, next_ref = refs[:7]
    left_refs = refs[7:]

    def store(piece, left, right, gate):
        right_ref[piece] = right
        next_ref[piece] = gate
        for number, left_ref in enumerate(left_refs):
            lanes = left_ref.shape[-1]
            left_ref[piece] = left[:, :, number * lanes : (number + 1) * lanes]

    values = tiles_of(tiles[:per])
    gate = gates[0][...].astype(jnp.float32)
    for part in range(1, parts):
        reached = pl.program_id(0) >= part * count
        values = jnp.where(reached, tiles_of(tiles[part * per : (part + 1) * per]), values)
        gate = jnp.where(reached, gates[part][...].astype(jnp.float32), gate)
    pair = updated(values, back_ref, gate, out_ref)
    pair_ref[...] = pair
    project(pair.astype(jnp.float32), wide_ref, mask_ref, store)


def last_kernel(pair_ref, back_ref, gate_ref, out_ref, final_ref):
    gate = gate_ref[...].astype(jnp.float32)
    pair = updated(pair_ref[...].astype(jnp.float32), back_ref, gate, out_ref)
    final_ref[...] = channel_norm(pair.astype(jnp.float32)).astype(final_ref.dtype)


def end_kernel(home_ref, hidden_ref, shared_ref, wide_ref, *refs):
    hidden = jnp.where(
        home_ref[0] == 1, hidden_ref[...].astype(jnp.float32), shared_ref[...].astype(jnp.float32)
    )
    refs[-1][...] = flat_dot(wide_ref[...], hidden).astype(refs[-1].dtype)


PARAMS = pltpu.CompilerParams(vmem_limit_bytes=48 << 20)


def cost(flops, moved_bytes):
    return pl.CostEstimate(flops=int(flops), bytes_accessed=int(moved_bytes), transcendentals=0)


def by_columns(shape):
    return pl.BlockSpec((shape[0], SUB, shape[2]), lambda w, *_: (0, w, 0))


def whole(shape):
    return pl.BlockSpec(shape, lambda w, *_: (0,) * len(shape))


def layer_of(shape, layer):
    return pl.BlockSpec((None, *shape[1:]), lambda w, *_: (layer,) + (0,) * (len(shape) - 1))


def tile_specs(got, per, place):
    def at(tile):
        def index(*position):
            number, column = place(*position[:-1])
            return position[-1][number * per + tile], 0, column, 0

        return pl.BlockSpec((None, got.shape[1], SUB, got.shape[3]), index)

    return [at(tile) for tile in range(per)]


def part_column(part, count):
    return lambda w: jnp.clip(w - part * count, 0, count - 1)


def stage(kernel, specs, out_shapes, ids, operands, flops):
    moved_bytes = sum(2 * shape.size for shape in out_shapes) * 2
    width = out_shapes[0].shape[1]
    return pl.pallas_call(
        kernel,
        grid_spec=pltpu.PrefetchScalarGridSpec(
            num_scalar_prefetch=1,
            grid=(width // SUB,),
            in_specs=specs,
            out_specs=[by_columns(shape.shape) for shape in out_shapes],
        ),
        out_shape=out_shapes,
        compiler_params=PARAMS,
        cost_estimate=cost(flops, moved_bytes),
    )(ids, *operands)


def first_stage(part, joint, ids, got, wide, mask):
    targets, channels, width, tile = got.shape
    per = ids.shape[0] // SPLIT
    lanes = per * tile
    count = width // SUB
    group = channels // targets
    lead, copies = ((targets, 2), 1) if joint else ((targets,), 2)
    zeros = (0,) * (len(lead) + 1)
    specs = tile_specs(got, per, lambda n, w: (n, w)) + [
        pl.BlockSpec((None, *wide.shape[1:]), lambda n, w, _: (0, 0, 0, 0)),
        pl.BlockSpec((SUB, lanes), lambda n, w, _: (part * count + w, n)),
    ]
    return pl.pallas_call(
        functools.partial(first_kernel, per),
        grid_spec=pltpu.PrefetchScalarGridSpec(
            num_scalar_prefetch=1,
            grid=(SPLIT, count),
            in_specs=specs,
            out_specs=[pl.BlockSpec((channels, SUB, lanes), lambda n, w, _: (0, w, n))]
            + [pl.BlockSpec((*lead, group, SUB, lanes), lambda n, w, _: (*zeros, w, n))] * copies,
        ),
        out_shape=[jax.ShapeDtypeStruct((channels, width, SPLIT * lanes), got.dtype)]
        + [jax.ShapeDtypeStruct((*lead, group, width, SPLIT * lanes), got.dtype)] * copies,
        compiler_params=PARAMS,
        cost_estimate=cost(
            2 * wide.size // NLAYER * count * SPLIT * lanes, 8 * channels * width * SPLIT * lanes
        ),
    )(ids, *[got] * per, wide, mask)


def middle_stage(layer, number, ids, gots, back, gates, out_wide, wide, mask):
    _, channels, width, tile = gots[0].shape
    per = ids.shape[0] // SPLIT
    lanes = per * tile
    count = width // SUB
    shape = jax.ShapeDtypeStruct((channels, width * len(gots), lanes), back.dtype)
    specs, operands = [], []
    for part, got in enumerate(gots):
        column = part_column(part, count)
        specs += tile_specs(got, per, lambda w, column=column: (number, column(w)))
        operands += [got] * per
    for part, gate in enumerate(gates):
        column = part_column(part, count)
        specs.append(
            pl.BlockSpec(
                (channels, SUB, lanes), lambda w, _, column=column: (0, column(w), number)
            )
        )
        operands.append(gate)
    specs += [
        by_columns(back.shape),
        layer_of(out_wide.shape, layer),
        layer_of(wide.shape, layer + 1),
        pl.BlockSpec((SUB, lanes), lambda w, _: (w, number)),
    ]
    operands += [back, out_wide, wide, mask]
    kernel = functools.partial(middle_kernel, len(gots), per, count)
    flops = 2 * (wide.size + out_wide.size) // NLAYER * count * len(gots) * lanes
    left = jax.ShapeDtypeStruct((*shape.shape[:2], lanes // LEFT_PARTS), back.dtype)
    return stage(kernel, specs, [shape] * 3 + [left] * LEFT_PARTS, ids, operands, flops)


def last_stage(layer, piece, pair, back, gate, out_wide):
    block = pl.BlockSpec((back.shape[0], SUB, back.shape[2]), lambda w: (0, w, piece))
    return pl.pallas_call(
        last_kernel,
        grid=(back.shape[1] // SUB,),
        in_specs=[block, by_columns(back.shape), block, layer_of(out_wide.shape, layer)],
        out_specs=by_columns(back.shape),
        out_shape=jax.ShapeDtypeStruct(back.shape, back.dtype),
        compiler_params=PARAMS,
        cost_estimate=cost(out_wide.size * back.size // CH // SUB, 8 * back.size),
    )(pair, back, gate, out_wide)


def end_stage(home, number, count, hidden, shared, wide, earlier):
    width, lanes = hidden.shape[1:]
    columns = wide.shape[0] // SUB
    out = jax.ShapeDtypeStruct((columns, width, lanes * count), hidden.dtype)
    specs = [by_columns(hidden.shape)] * 2 + [whole(wide.shape)]
    operands = [hidden, shared, wide]
    if earlier is not None:
        specs.append(pl.BlockSpec(memory_space=pl.ANY))
        operands.append(earlier)
    return pl.pallas_call(
        end_kernel,
        grid_spec=pltpu.PrefetchScalarGridSpec(
            num_scalar_prefetch=1,
            grid=(width // SUB,),
            in_specs=specs,
            out_specs=pl.BlockSpec((columns, SUB, lanes), lambda w, _: (0, w, number)),
        ),
        out_shape=out,
        input_output_aliases={} if earlier is None else {4: 0},
        compiler_params=PARAMS,
        cost_estimate=cost(2 * wide.size * width // SUB * lanes, 8 * hidden.size),
    )(home, *operands)


def product_kernel(axis, count, *refs):
    lefts, rights, out_ref = refs[:count], refs[count:-1], refs[-1]
    targets, _, width, chunk = out_ref.shape

    def matrix(ref):
        value = ref[...]
        return value.reshape(value.shape[0] * value.shape[-2], value.shape[-1])

    def times(left, right):
        return lax.dot_general(
            right, left, (((0,), (0,)), ((), ())), preferred_element_type=jnp.float32
        )

    if axis == "depth":
        left = jnp.concatenate([matrix(ref) for ref in lefts], axis=0)
        right = jnp.concatenate([matrix(ref) for ref in rights], axis=0)
        pieces = [times(left, right)]
    else:
        pieces = [times(matrix(lefts[0]), matrix(right)) for right in rights]
    per = targets // len(pieces)
    for number, piece in enumerate(pieces):
        out_ref[number * per : (number + 1) * per] = piece.astype(out_ref.dtype).reshape(
            per, 1, width, chunk
        )


def product_call(axis, specs, operands, count, out):
    targets, channels, width, chunk = out.shape
    return pl.pallas_call(
        functools.partial(product_kernel, axis, count),
        grid=(channels,),
        in_specs=specs,
        out_specs=pl.BlockSpec((targets, 1, width, chunk), lambda c: (0, c, 0, 0)),
        out_shape=out,
        compiler_params=pltpu.CompilerParams(vmem_limit_bytes=40 << 20),
        cost_estimate=cost(2 * out.size * targets * width, 8 * out.size),
    )(*operands)


def depth_products(number, boths, chunk):
    targets, channels = boths[0][0].shape[0], boths[0][0].shape[-3]
    specs, operands, depth = [], [], 0
    for side in range(2):
        for arrays in boths:
            width, lanes = arrays[0].shape[-2:]
            size, place = (lanes, 0) if side else (chunk, number)
            if len(arrays) == 1:
                spec = pl.BlockSpec(
                    (targets, None, 1, width, size),
                    lambda c, side=side, place=place: (0, side, c, 0, place),
                )
            else:
                spec = pl.BlockSpec(
                    (targets, 1, width, size), lambda c, place=place: (0, c, 0, place)
                )
            specs.append(spec)
            operands.append(arrays[0] if len(arrays) == 1 else arrays[side])
            depth += (1 - side) * width
    out = jax.ShapeDtypeStruct((targets, channels, depth, chunk), operands[0].dtype)
    return product_call("depth", specs, operands, len(boths), out)


def row_products(left, rights):
    targets, _, width, _ = left.shape

    def spec(array):
        return pl.BlockSpec((targets, 1, width, array.shape[3]), lambda c: (0, c, 0, 0))

    out = jax.ShapeDtypeStruct(left.shape, left.dtype)
    specs = [spec(array) for array in (left, *rights)]
    return product_call("rows", specs, [left, *rights], 1, out)


def pack_kernel(ids_ref, rows_ref, packed_ref):
    rows = rows_ref[...].astype(jnp.float32)
    packed_ref[...] = jnp.swapaxes(jnp.swapaxes(rows, 0, 1), 1, 2).astype(packed_ref.dtype)


def pack(ids, rows):
    tile, channels, _ = rows.shape
    slots = ids.shape[0]
    group = 2 * SUB
    out = jax.ShapeDtypeStruct((channels, slots * TILE, tile), rows.dtype)
    return pl.pallas_call(
        pack_kernel,
        grid_spec=pltpu.PrefetchScalarGridSpec(
            num_scalar_prefetch=1,
            grid=(slots, channels // group),
            in_specs=[pl.BlockSpec((tile, group, TILE), lambda s, c, ids: (0, c, ids[s]))],
            out_specs=pl.BlockSpec((group, TILE, tile), lambda s, c, ids: (c, s, 0)),
        ),
        out_shape=out,
        compiler_params=PARAMS,
        cost_estimate=cost(0, 4 * out.size),
    )(ids, rows)


def spread_kernel(part, send_ref, got_ref, hold, send_sem, recv_sem, hold_sem):
    columns = pl.ds(part * got_ref.shape[2], got_ref.shape[2])
    core, half, inner = (lax.axis_index(name) for name in ("core", "half", "inner"))
    cores, halves, width = (lax.axis_size(name) for name in ("core", "half", "inner"))
    blocks = cores * width
    row = half * width + inner
    mine = core * width + inner
    barrier = pltpu.get_barrier_semaphore()
    total = cores * halves * width
    flat = (core * halves + half) * width + inner
    for step in range(1, total):
        other = lax.rem(flat + step, total)
        pl.semaphore_signal(
            barrier,
            inc=1,
            device_id={
                "core": other // (halves * width),
                "half": lax.rem(other // width, halves),
                "inner": lax.rem(other, width),
            },
            device_id_type=pl.DeviceIdType.MESH,
        )
    pl.semaphore_wait(barrier, total - 1)

    def outgoing(step):
        block = lax.rem(mine + step, blocks)
        return pltpu.make_async_remote_copy(
            src_ref=send_ref.at[:, block, columns],
            dst_ref=got_ref.at[row],
            send_sem=send_sem.at[step],
            recv_sem=recv_sem.at[row],
            device_id={"core": block // width, "half": core, "inner": lax.rem(block, width)},
            device_id_type=pl.DeviceIdType.MESH,
        )

    home = half == core
    for step in range(1, blocks):
        outgoing(step).start()

    @pl.when(home)
    def _():
        bring = pltpu.make_async_copy(send_ref.at[:, mine, columns], hold, hold_sem.at[0])
        bring.start()
        bring.wait()
        put = pltpu.make_async_copy(hold, got_ref.at[row], hold_sem.at[1])
        put.start()
        put.wait()

    @pl.when(jnp.logical_not(home))
    def _():
        outgoing(0).start()

    def incoming(slot):
        return pltpu.make_async_remote_copy(
            src_ref=send_ref.at[:, 0, columns],
            dst_ref=got_ref.at[slot],
            send_sem=send_sem.at[0],
            recv_sem=recv_sem.at[slot],
            device_id={"core": core, "half": half, "inner": inner},
            device_id_type=pl.DeviceIdType.MESH,
        )

    for step in range(1, blocks):
        outgoing(step).wait_send()

    @pl.when(jnp.logical_not(home))
    def _():
        outgoing(0).wait_send()

    for step in range(1, blocks):
        incoming(lax.rem(row + step, blocks)).wait_recv()

    @pl.when(jnp.logical_not(home))
    def _():
        incoming(row).wait_recv()


def spread(send, part):
    channels, blocks, width, tile = send.shape
    width = width // COLUMN_PARTS
    return pl.pallas_call(
        functools.partial(spread_kernel, part),
        in_specs=[pl.BlockSpec(memory_space=pl.ANY)],
        out_specs=pl.BlockSpec(memory_space=pl.ANY),
        out_shape=jax.ShapeDtypeStruct((blocks, channels, width, tile), send.dtype),
        scratch_shapes=[
            pltpu.VMEM((channels, width, tile), send.dtype),
            pltpu.SemaphoreType.DMA((blocks,)),
            pltpu.SemaphoreType.DMA((blocks,)),
            pltpu.SemaphoreType.DMA((2,)),
        ],
        compiler_params=pltpu.CompilerParams(
            collective_id=part, has_side_effects=True, vmem_limit_bytes=32 << 20
        ),
        cost_estimate=cost(0, 64 * blocks * channels * width * tile),
    )(send)


GROUP = ("core", "inner")


def exchange(value):
    return lax.all_to_all(value, GROUP, split_axis=0, concat_axis=0, tiled=True)


def moved(value, pairs):
    halves = lax.axis_size("half")
    steps = [(a * halves + b, c * halves + d) for (a, b), (c, d) in pairs]
    return lax.ppermute(value, ("core", "half"), steps)


def after(value, *others):
    return lax.optimization_barrier((value, *others))[0]


def in_halves(pair_maps, crop_tiles, full_length, proj_weight, out_weight, final_weight):
    cores, halves, inner_count = (lax.axis_size(name) for name in ("core", "half", "inner"))
    core, half, inner = (lax.axis_index(name) for name in ("core", "half", "inner"))
    row_count = cores * inner_count
    my_index = core * inner_count + inner
    col_width = CROP // row_count
    per_group = CH // row_count
    chunk = CROP // SPLIT
    held_ids = crop_tiles[0]
    other_ids = lax.ppermute(held_ids, "core", [(0, 1), (1, 0)])
    crop_ids = jnp.where(core == half, held_ids, other_ids)
    position = crop_ids[:, None] * TILE + jnp.arange(TILE, dtype=jnp.int32)
    usable = (position < full_length[0]).astype(jnp.float32).reshape(CROP)
    col_usable = lax.dynamic_slice_in_dim(usable, my_index * col_width, col_width)
    pair_mask = col_usable[:, None] * usable[None, :]
    send = pack(held_ids, jnp.transpose(pair_maps[0], (0, 2, 1)))
    send = send.reshape(CH, row_count, col_width, TILE)
    wides, outs, final_wide = widen(proj_weight, out_weight, final_weight)
    gots, gates, boths = [], [], []
    for part in range(COLUMN_PARTS):
        got = spread(send, part)
        joint = part + 1 < COLUMN_PARTS
        gate, *sends = first_stage(part, joint, crop_ids, got, wides, pair_mask)
        send = after(send, sends[0])
        gots.append(got)
        gates.append(gate)
        arrays = []
        for value in sends:
            arrays.append(exchange(value))
        boths.append(arrays)
    following = []
    for number in range(SPLIT):
        merged = exchange(depth_products(number, boths, chunk)).reshape(CH, col_width, chunk)
        following.append(
            middle_stage(0, number, crop_ids, gots, merged, gates, outs, wides, pair_mask)
        )
    rights = []
    for item in following:
        rights.append(exchange(item[1].reshape(row_count, per_group, col_width, chunk)))
    ready, arrived = [], []
    back = None
    for pair, _, gate, *lefts in following:
        for piece, left in enumerate(lefts):
            left = left.reshape(row_count, per_group, col_width, chunk // LEFT_PARTS)
            left = exchange(left if back is None else after(left, back, ready[-1]))
            back = exchange(row_products(left, rights))
            merged = back.reshape(CH, col_width, chunk // LEFT_PARTS)
            ready.append(last_stage(NLAYER - 1, piece, pair, merged, gate, outs))
            arrived.append(moved(ready[-1], [((0, 1), (0, 0)), ((1, 0), (1, 1))]))
    hiddens, shareds = [], []
    for normed_final, across in zip(ready, arrived):
        summed = normed_final.astype(jnp.float32) + across.astype(jnp.float32)
        hiddens.append(jnp.maximum(summed / halves, 0.0).astype(jnp.bfloat16))
        shareds.append(moved(hiddens[-1], [((0, 0), (1, 0)), ((1, 1), (0, 1))]))
    home = (core == half).astype(jnp.int32)[None]
    result = None
    for number, (hidden, shared) in enumerate(zip(hiddens, shareds)):
        result = end_stage(home, number, len(hiddens), hidden, shared, final_wide, result)
    return result


def on_device(pair_maps, crop_tiles, full_length, proj_weight, out_weight, final_weight):
    row_count = lax.axis_size("row")
    my_index = lax.axis_index("row")
    pair_local = pair_maps[0]
    crop_ids = crop_tiles[0]
    local_rows = pair_local.shape[0]
    col_width = CROP // row_count
    parts_count = max(1, row_count // CH)
    per_group = CH * parts_count // row_count
    groups = CH // per_group
    part_rows = CROP // parts_count
    steps_crop = jnp.arange(CROP, dtype=jnp.int32)
    position = crop_ids[steps_crop // TILE] * TILE + steps_crop % TILE
    usable = (position < full_length[0]).astype(jnp.float32)
    col_usable = lax.dynamic_slice_in_dim(usable, my_index * col_width, col_width)
    pair_mask = col_usable[:, None] * usable[None, :]
    columns = pair_local.reshape(local_rows, FULL // TILE, TILE, CH)[:, crop_ids]
    columns = columns.reshape(local_rows, CROP * CH)
    received = lax.all_to_all(columns, "row", split_axis=1, concat_axis=0, tiled=True)
    cropped = received.reshape(FULL // TILE, TILE, col_width * CH)[crop_ids]
    current = jnp.transpose(cropped.reshape(CROP, col_width, CH), (2, 1, 0))
    for layer_idx in range(NLAYER):
        normed_in = channel_norm(current.astype(jnp.float32)).astype(jnp.bfloat16)
        projected = jnp.einsum(
            "cd,cwi->dwi", proj_weight[layer_idx], normed_in, preferred_element_type=jnp.float32
        )
        left_proj = (jax.nn.sigmoid(projected[:CH]) * projected[CH : 2 * CH] * pair_mask).astype(
            jnp.bfloat16
        )
        right_proj = (
            jax.nn.sigmoid(projected[2 * CH : 3 * CH]) * projected[3 * CH : 4 * CH] * pair_mask
        ).astype(jnp.bfloat16)
        gate_vals = jax.nn.sigmoid(projected[4 * CH :])
        left_send = left_proj.reshape(groups, per_group, col_width, parts_count, part_rows)
        left_send = jnp.transpose(left_send, (0, 3, 1, 2, 4)).reshape(
            row_count, per_group, col_width, part_rows
        )
        right_send = right_proj.reshape(groups, per_group, col_width, parts_count, part_rows)
        right_send = jnp.transpose(right_send, (0, 3, 1, 2, 4)).reshape(
            row_count, per_group, col_width, part_rows
        )
        left_got, right_got = (
            lax.all_to_all(left_send, "row", split_axis=0, concat_axis=2, tiled=True),
            lax.all_to_all(right_send, "row", split_axis=0, concat_axis=2, tiled=True),
        )
        right_whole = right_got[0]
        for bit_pos in range(parts_count.bit_length() - 1):
            partner = from_partner(right_whole, "row", bit_pos)
            lower_side = my_index // (1 << bit_pos) % 2 == 0
            right_whole = jnp.where(
                lower_side,
                jnp.concatenate([right_whole, partner], axis=2),
                jnp.concatenate([partner, right_whole], axis=2),
            )
        products = jnp.einsum(
            "cki,ckj->cij", left_got[0], right_whole, preferred_element_type=jnp.float32
        ).astype(jnp.bfloat16)
        back_send = jnp.transpose(
            products.reshape(per_group, part_rows, row_count, col_width), (2, 0, 3, 1)
        )
        back_got = lax.all_to_all(back_send, "row", split_axis=0, concat_axis=0, tiled=True)
        merged = back_got.reshape(groups, parts_count, per_group, col_width, part_rows)
        merged = jnp.transpose(merged, (0, 2, 3, 1, 4)).reshape(CH, col_width, CROP)
        normed_out = channel_norm(merged.astype(jnp.float32)).astype(jnp.bfloat16)
        update = jnp.einsum(
            "cd,cwi->dwi", out_weight[layer_idx], normed_out, preferred_element_type=jnp.float32
        )
        current = (current.astype(jnp.float32) + gate_vals * update).astype(jnp.bfloat16)
    normed_final = channel_norm(current.astype(jnp.float32))
    template_count = lax.axis_size("tmpl")
    summed = lax.psum(normed_final.astype(jnp.bfloat16), "tmpl").astype(jnp.float32)
    hidden = jnp.maximum(summed / template_count, 0.0).astype(jnp.bfloat16)
    result = jnp.einsum(
        "cz,cwi->zwi", final_weight, hidden, preferred_element_type=jnp.float32
    ).astype(jnp.bfloat16)
    return result


def solution(mesh):
    rows, templates = mesh.shape["row"], mesh.shape["tmpl"]
    whole_tiles = FULL // rows == TILE and CH % rows == 0
    if whole_tiles and templates == 2:
        grid = Mesh(
            mesh.devices.reshape(templates, templates, rows // templates),
            ("core", "half", "inner"),
        )
        lines = ("half", "inner")
        placed = (P("core", lines, None, None), P("core", None), P(), P(), P(), P())
        return jax.shard_map(
            in_halves, mesh=grid, in_specs=placed, out_specs=P(None, lines, None), check_vma=False
        )
    placed = (P("tmpl", "row", None, None), P("tmpl", None), P(), P(), P(), P())
    return jax.shard_map(
        on_device, mesh=mesh, in_specs=placed, out_specs=P(None, "row", None), check_vma=False
    )
```

```python
import functools

import jax
import jax.numpy as jnp
from jax import lax
from jax.experimental import pallas as pl
from jax.experimental.pallas import tpu as pltpu
from jax.sharding import Mesh, PartitionSpec as P

CH = 64
CROP = 1024
TILE = 128
NLAYER = 2
FULL = 2048


EPSILON = 1e-05


def from_partner(value, axis, bit):
    mask = 2**bit
    pairs = [(source, source ^ mask) for source in range(lax.axis_size(axis))]
    return lax.ppermute(value, axis, pairs)


def channel_norm(values):
    center = values - jnp.mean(values, axis=0, keepdims=True)
    spread = jnp.mean(center * center, axis=0, keepdims=True)
    return center * lax.rsqrt(spread + EPSILON)


SPLIT = 2
SUB = 8
PARTS = 2
COLUMN_PARTS = 2
LEFT_PARTS = 1


def widened(weight, source):
    depth, columns = weight.shape
    size = source.shape[0]
    pick = (source == lax.broadcasted_iota(jnp.int32, (size, columns), 1)).astype(weight.dtype)
    taken = lax.dot_general(
        pick, weight, (((1,), (1,)), ((), ())), preferred_element_type=jnp.float32
    ).astype(weight.dtype)
    grow = lax.broadcasted_iota(jnp.int32, (depth, depth * SUB), 1) // SUB
    grow = (grow == lax.broadcasted_iota(jnp.int32, grow.shape, 0)).astype(weight.dtype)
    wide = jnp.dot(taken, grow, preferred_element_type=jnp.float32)
    row = lax.broadcasted_iota(jnp.int32, wide.shape, 0) % SUB
    lane = lax.broadcasted_iota(jnp.int32, wide.shape, 1) % SUB
    return jnp.where(row == lane, wide, 0.0).astype(weight.dtype)


def widen_kernel(proj_ref, out_ref, final_ref, wide_ref, out_wide_ref, final_wide_ref):
    size = CH // PARTS
    for layer in range(NLAYER):
        for part in range(PARTS):
            rows = lax.broadcasted_iota(jnp.int32, (5 * size * SUB, 5 * CH), 0) // SUB
            source = rows // size * CH + part * size + rows % size
            wide_ref[layer, part] = widened(proj_ref[layer], source)
        rows = lax.broadcasted_iota(jnp.int32, (CH * SUB, CH), 0) // SUB
        out_wide_ref[layer] = widened(out_ref[layer], rows)
    columns = final_ref.shape[1]
    rows = lax.broadcasted_iota(jnp.int32, (columns * SUB, columns), 0) // SUB
    final_wide_ref[...] = widened(final_ref[...], rows)


def widen(proj_weight, out_weight, final_weight):
    kind = proj_weight.dtype
    return pl.pallas_call(
        widen_kernel,
        out_shape=[
            jax.ShapeDtypeStruct((NLAYER, PARTS, 5 * CH // PARTS * SUB, CH * SUB), kind),
            jax.ShapeDtypeStruct((NLAYER, CH * SUB, CH * SUB), kind),
            jax.ShapeDtypeStruct((final_weight.shape[1] * SUB, CH * SUB), kind),
        ],
        compiler_params=PARAMS,
    )(proj_weight, out_weight, final_weight)


def sigmoid(values):
    return 0.5 * jnp.tanh(0.5 * values) + 0.5


def flat_dot(weight, values):
    channels, sub, lanes = values.shape
    return jnp.dot(
        weight,
        values.reshape(channels * sub, lanes).astype(jnp.bfloat16),
        preferred_element_type=jnp.float32,
    ).reshape(weight.shape[0] // sub, sub, lanes)


def project(values, wide_ref, mask_ref, store):
    normed = channel_norm(values)
    mask = mask_ref[...][None]
    size = CH // PARTS
    for part in range(PARTS):
        projected = flat_dot(wide_ref[part], normed)
        left = sigmoid(projected[:size]) * projected[size : 2 * size] * mask
        right = sigmoid(projected[2 * size : 3 * size]) * projected[3 * size : 4 * size] * mask
        gate = sigmoid(projected[4 * size :])
        pieces = [item.astype(jnp.bfloat16) for item in (left, right, gate)]
        store(slice(part * size, (part + 1) * size), *pieces)


def updated(values, back_ref, gate, out_ref):
    normed = channel_norm(back_ref[...].astype(jnp.float32))
    update = flat_dot(out_ref[...], normed)
    return (values + gate * update).astype(jnp.bfloat16)


def tiles_of(refs):
    return jnp.concatenate([ref[...].astype(jnp.float32) for ref in refs], axis=-1)


def first_kernel(per, ids_ref, *refs):
    wide_ref, mask_ref, gate_ref, *send_refs = refs[per:]
    group, sub, lanes = send_refs[0].shape[-3:]

    def store(piece, left, right, gate):
        place = slice(piece.start // group, piece.stop // group)
        for side, value in enumerate((left, right)):
            value = value.reshape(-1, group, sub, lanes)
            if len(send_refs) == 1:
                send_refs[0][place, side] = value
            else:
                send_refs[side][place] = value
        gate_ref[piece] = gate

    project(tiles_of(refs[:per]), wide_ref, mask_ref, store)


def middle_kernel(parts, per, count, ids_ref, *refs):
    tiles, refs = refs[: parts * per], refs[parts * per :]
    gates, refs = refs[:parts], refs[parts:]
    back_ref, out_ref, wide_ref, mask_ref, pair_ref, right_ref, next_ref = refs[:7]
    left_refs = refs[7:]

    def store(piece, left, right, gate):
        right_ref[piece] = right
        next_ref[piece] = gate
        for number, left_ref in enumerate(left_refs):
            lanes = left_ref.shape[-1]
            left_ref[piece] = left[:, :, number * lanes : (number + 1) * lanes]

    values = tiles_of(tiles[:per])
    gate = gates[0][...].astype(jnp.float32)
    for part in range(1, parts):
        reached = pl.program_id(0) >= part * count
        values = jnp.where(reached, tiles_of(tiles[part * per : (part + 1) * per]), values)
        gate = jnp.where(reached, gates[part][...].astype(jnp.float32), gate)
    pair = updated(values, back_ref, gate, out_ref)
    pair_ref[...] = pair
    project(pair.astype(jnp.float32), wide_ref, mask_ref, store)


def last_kernel(pair_ref, back_ref, gate_ref, out_ref, final_ref):
    gate = gate_ref[...].astype(jnp.float32)
    pair = updated(pair_ref[...].astype(jnp.float32), back_ref, gate, out_ref)
    final_ref[...] = channel_norm(pair.astype(jnp.float32)).astype(final_ref.dtype)


def end_kernel(home_ref, hidden_ref, shared_ref, wide_ref, *refs):
    hidden = jnp.where(
        home_ref[0] == 1, hidden_ref[...].astype(jnp.float32), shared_ref[...].astype(jnp.float32)
    )
    refs[-1][...] = flat_dot(wide_ref[...], hidden).astype(refs[-1].dtype)


PARAMS = pltpu.CompilerParams(vmem_limit_bytes=48 << 20)


def cost(flops, moved_bytes):
    return pl.CostEstimate(flops=int(flops), bytes_accessed=int(moved_bytes), transcendentals=0)


def by_columns(shape):
    return pl.BlockSpec((shape[0], SUB, shape[2]), lambda w, *_: (0, w, 0))


def whole(shape):
    return pl.BlockSpec(shape, lambda w, *_: (0,) * len(shape))


def layer_of(shape, layer):
    return pl.BlockSpec((None, *shape[1:]), lambda w, *_: (layer,) + (0,) * (len(shape) - 1))


def tile_specs(got, per, place):
    def at(tile):
        def index(*position):
            number, column = place(*position[:-1])
            return position[-1][number * per + tile], 0, column, 0

        return pl.BlockSpec((None, got.shape[1], SUB, got.shape[3]), index)

    return [at(tile) for tile in range(per)]


def part_column(part, count):
    return lambda w: jnp.clip(w - part * count, 0, count - 1)


def stage(kernel, specs, out_shapes, ids, operands, flops):
    moved_bytes = sum(2 * shape.size for shape in out_shapes) * 2
    width = out_shapes[0].shape[1]
    return pl.pallas_call(
        kernel,
        grid_spec=pltpu.PrefetchScalarGridSpec(
            num_scalar_prefetch=1,
            grid=(width // SUB,),
            in_specs=specs,
            out_specs=[by_columns(shape.shape) for shape in out_shapes],
        ),
        out_shape=out_shapes,
        compiler_params=PARAMS,
        cost_estimate=cost(flops, moved_bytes),
    )(ids, *operands)


def first_stage(part, joint, ids, got, wide, mask):
    targets, channels, width, tile = got.shape
    per = ids.shape[0] // SPLIT
    lanes = per * tile
    count = width // SUB
    group = channels // targets
    lead, copies = ((targets, 2), 1) if joint else ((targets,), 2)
    zeros = (0,) * (len(lead) + 1)
    specs = tile_specs(got, per, lambda n, w: (n, w)) + [
        pl.BlockSpec((None, *wide.shape[1:]), lambda n, w, _: (0, 0, 0, 0)),
        pl.BlockSpec((SUB, lanes), lambda n, w, _: (part * count + w, n)),
    ]
    return pl.pallas_call(
        functools.partial(first_kernel, per),
        grid_spec=pltpu.PrefetchScalarGridSpec(
            num_scalar_prefetch=1,
            grid=(SPLIT, count),
            in_specs=specs,
            out_specs=[pl.BlockSpec((channels, SUB, lanes), lambda n, w, _: (0, w, n))]
            + [pl.BlockSpec((*lead, group, SUB, lanes), lambda n, w, _: (*zeros, w, n))] * copies,
        ),
        out_shape=[jax.ShapeDtypeStruct((channels, width, SPLIT * lanes), got.dtype)]
        + [jax.ShapeDtypeStruct((*lead, group, width, SPLIT * lanes), got.dtype)] * copies,
        compiler_params=PARAMS,
        cost_estimate=cost(
            2 * wide.size // NLAYER * count * SPLIT * lanes, 8 * channels * width * SPLIT * lanes
        ),
    )(ids, *[got] * per, wide, mask)


def middle_stage(layer, number, ids, gots, back, gates, out_wide, wide, mask):
    _, channels, width, tile = gots[0].shape
    per = ids.shape[0] // SPLIT
    lanes = per * tile
    count = width // SUB
    shape = jax.ShapeDtypeStruct((channels, width * len(gots), lanes), back.dtype)
    specs, operands = [], []
    for part, got in enumerate(gots):
        column = part_column(part, count)
        specs += tile_specs(got, per, lambda w, column=column: (number, column(w)))
        operands += [got] * per
    for part, gate in enumerate(gates):
        column = part_column(part, count)
        specs.append(
            pl.BlockSpec(
                (channels, SUB, lanes), lambda w, _, column=column: (0, column(w), number)
            )
        )
        operands.append(gate)
    specs += [
        by_columns(back.shape),
        layer_of(out_wide.shape, layer),
        layer_of(wide.shape, layer + 1),
        pl.BlockSpec((SUB, lanes), lambda w, _: (w, number)),
    ]
    operands += [back, out_wide, wide, mask]
    kernel = functools.partial(middle_kernel, len(gots), per, count)
    flops = 2 * (wide.size + out_wide.size) // NLAYER * count * len(gots) * lanes
    left = jax.ShapeDtypeStruct((*shape.shape[:2], lanes // LEFT_PARTS), back.dtype)
    return stage(kernel, specs, [shape] * 3 + [left] * LEFT_PARTS, ids, operands, flops)


def last_stage(layer, piece, pair, back, gate, out_wide):
    block = pl.BlockSpec((back.shape[0], SUB, back.shape[2]), lambda w: (0, w, piece))
    return pl.pallas_call(
        last_kernel,
        grid=(back.shape[1] // SUB,),
        in_specs=[block, by_columns(back.shape), block, layer_of(out_wide.shape, layer)],
        out_specs=by_columns(back.shape),
        out_shape=jax.ShapeDtypeStruct(back.shape, back.dtype),
        compiler_params=PARAMS,
        cost_estimate=cost(out_wide.size * back.size // CH // SUB, 8 * back.size),
    )(pair, back, gate, out_wide)


def end_stage(home, number, count, hidden, shared, wide, earlier):
    width, lanes = hidden.shape[1:]
    columns = wide.shape[0] // SUB
    out = jax.ShapeDtypeStruct((columns, width, lanes * count), hidden.dtype)
    specs = [by_columns(hidden.shape)] * 2 + [whole(wide.shape)]
    operands = [hidden, shared, wide]
    if earlier is not None:
        specs.append(pl.BlockSpec(memory_space=pl.ANY))
        operands.append(earlier)
    return pl.pallas_call(
        end_kernel,
        grid_spec=pltpu.PrefetchScalarGridSpec(
            num_scalar_prefetch=1,
            grid=(width // SUB,),
            in_specs=specs,
            out_specs=pl.BlockSpec((columns, SUB, lanes), lambda w, _: (0, w, number)),
        ),
        out_shape=out,
        input_output_aliases={} if earlier is None else {4: 0},
        compiler_params=PARAMS,
        cost_estimate=cost(2 * wide.size * width // SUB * lanes, 8 * hidden.size),
    )(home, *operands)


def product_kernel(axis, count, *refs):
    lefts, rights, out_ref = refs[:count], refs[count:-1], refs[-1]
    targets, _, width, chunk = out_ref.shape

    def matrix(ref):
        value = ref[...]
        return value.reshape(value.shape[0] * value.shape[-2], value.shape[-1])

    def times(left, right):
        return lax.dot_general(
            right, left, (((0,), (0,)), ((), ())), preferred_element_type=jnp.float32
        )

    if axis == "depth":
        left = jnp.concatenate([matrix(ref) for ref in lefts], axis=0)
        right = jnp.concatenate([matrix(ref) for ref in rights], axis=0)
        pieces = [times(left, right)]
    else:
        pieces = [times(matrix(lefts[0]), matrix(right)) for right in rights]
    per = targets // len(pieces)
    for number, piece in enumerate(pieces):
        out_ref[number * per : (number + 1) * per] = piece.astype(out_ref.dtype).reshape(
            per, 1, width, chunk
        )


def product_call(axis, specs, operands, count, out):
    targets, channels, width, chunk = out.shape
    return pl.pallas_call(
        functools.partial(product_kernel, axis, count),
        grid=(channels,),
        in_specs=specs,
        out_specs=pl.BlockSpec((targets, 1, width, chunk), lambda c: (0, c, 0, 0)),
        out_shape=out,
        compiler_params=pltpu.CompilerParams(vmem_limit_bytes=40 << 20),
        cost_estimate=cost(2 * out.size * targets * width, 8 * out.size),
    )(*operands)


def depth_products(number, boths, chunk):
    targets, channels = boths[0][0].shape[0], boths[0][0].shape[-3]
    specs, operands, depth = [], [], 0
    for side in range(2):
        for arrays in boths:
            width, lanes = arrays[0].shape[-2:]
            size, place = (lanes, 0) if side else (chunk, number)
            if len(arrays) == 1:
                spec = pl.BlockSpec(
                    (targets, None, 1, width, size),
                    lambda c, side=side, place=place: (0, side, c, 0, place),
                )
            else:
                spec = pl.BlockSpec(
                    (targets, 1, width, size), lambda c, place=place: (0, c, 0, place)
                )
            specs.append(spec)
            operands.append(arrays[0] if len(arrays) == 1 else arrays[side])
            depth += (1 - side) * width
    out = jax.ShapeDtypeStruct((targets, channels, depth, chunk), operands[0].dtype)
    return product_call("depth", specs, operands, len(boths), out)


def row_products(left, rights):
    targets, _, width, _ = left.shape

    def spec(array):
        return pl.BlockSpec((targets, 1, width, array.shape[3]), lambda c: (0, c, 0, 0))

    out = jax.ShapeDtypeStruct(left.shape, left.dtype)
    specs = [spec(array) for array in (left, *rights)]
    return product_call("rows", specs, [left, *rights], 1, out)


def pack_kernel(ids_ref, rows_ref, packed_ref):
    rows = rows_ref[...].astype(jnp.float32)
    packed_ref[...] = jnp.swapaxes(jnp.swapaxes(rows, 0, 1), 1, 2).astype(packed_ref.dtype)


def pack(ids, rows):
    tile, channels, _ = rows.shape
    slots = ids.shape[0]
    group = 2 * SUB
    out = jax.ShapeDtypeStruct((channels, slots * TILE, tile), rows.dtype)
    return pl.pallas_call(
        pack_kernel,
        grid_spec=pltpu.PrefetchScalarGridSpec(
            num_scalar_prefetch=1,
            grid=(slots, channels // group),
            in_specs=[pl.BlockSpec((tile, group, TILE), lambda s, c, ids: (0, c, ids[s]))],
            out_specs=pl.BlockSpec((group, TILE, tile), lambda s, c, ids: (c, s, 0)),
        ),
        out_shape=out,
        compiler_params=PARAMS,
        cost_estimate=cost(0, 4 * out.size),
    )(ids, rows)


def spread_kernel(part, send_ref, got_ref, hold, send_sem, recv_sem, hold_sem):
    columns = pl.ds(part * got_ref.shape[2], got_ref.shape[2])
    core, half, inner = (lax.axis_index(name) for name in ("core", "half", "inner"))
    cores, halves, width = (lax.axis_size(name) for name in ("core", "half", "inner"))
    blocks = cores * width
    row = half * width + inner
    mine = core * width + inner
    barrier = pltpu.get_barrier_semaphore()
    total = cores * halves * width
    flat = (core * halves + half) * width + inner
    for step in range(1, total):
        other = lax.rem(flat + step, total)
        pl.semaphore_signal(
            barrier,
            inc=1,
            device_id={
                "core": other // (halves * width),
                "half": lax.rem(other // width, halves),
                "inner": lax.rem(other, width),
            },
            device_id_type=pl.DeviceIdType.MESH,
        )
    pl.semaphore_wait(barrier, total - 1)

    def outgoing(step):
        block = lax.rem(mine + step, blocks)
        return pltpu.make_async_remote_copy(
            src_ref=send_ref.at[:, block, columns],
            dst_ref=got_ref.at[row],
            send_sem=send_sem.at[step],
            recv_sem=recv_sem.at[row],
            device_id={"core": block // width, "half": core, "inner": lax.rem(block, width)},
            device_id_type=pl.DeviceIdType.MESH,
        )

    home = half == core
    for step in range(1, blocks):
        outgoing(step).start()

    @pl.when(home)
    def _():
        bring = pltpu.make_async_copy(send_ref.at[:, mine, columns], hold, hold_sem.at[0])
        bring.start()
        bring.wait()
        put = pltpu.make_async_copy(hold, got_ref.at[row], hold_sem.at[1])
        put.start()
        put.wait()

    @pl.when(jnp.logical_not(home))
    def _():
        outgoing(0).start()

    def incoming(slot):
        return pltpu.make_async_remote_copy(
            src_ref=send_ref.at[:, 0, columns],
            dst_ref=got_ref.at[slot],
            send_sem=send_sem.at[0],
            recv_sem=recv_sem.at[slot],
            device_id={"core": core, "half": half, "inner": inner},
            device_id_type=pl.DeviceIdType.MESH,
        )

    for step in range(1, blocks):
        outgoing(step).wait_send()

    @pl.when(jnp.logical_not(home))
    def _():
        outgoing(0).wait_send()

    for step in range(1, blocks):
        incoming(lax.rem(row + step, blocks)).wait_recv()

    @pl.when(jnp.logical_not(home))
    def _():
        incoming(row).wait_recv()


def spread(send, part):
    channels, blocks, width, tile = send.shape
    width = width // COLUMN_PARTS
    return pl.pallas_call(
        functools.partial(spread_kernel, part),
        in_specs=[pl.BlockSpec(memory_space=pl.ANY)],
        out_specs=pl.BlockSpec(memory_space=pl.ANY),
        out_shape=jax.ShapeDtypeStruct((blocks, channels, width, tile), send.dtype),
        scratch_shapes=[
            pltpu.VMEM((channels, width, tile), send.dtype),
            pltpu.SemaphoreType.DMA((blocks,)),
            pltpu.SemaphoreType.DMA((blocks,)),
            pltpu.SemaphoreType.DMA((2,)),
        ],
        compiler_params=pltpu.CompilerParams(
            collective_id=part, has_side_effects=True, vmem_limit_bytes=32 << 20
        ),
        cost_estimate=cost(0, 64 * blocks * channels * width * tile),
    )(send)


GROUP = ("core", "inner")


def exchange(value):
    return lax.all_to_all(value, GROUP, split_axis=0, concat_axis=0, tiled=True)


def moved(value, pairs):
    halves = lax.axis_size("half")
    steps = [(a * halves + b, c * halves + d) for (a, b), (c, d) in pairs]
    return lax.ppermute(value, ("core", "half"), steps)


def after(value, *others):
    return lax.optimization_barrier((value, *others))[0]


def in_halves(pair_maps, crop_tiles, full_length, proj_weight, out_weight, final_weight):
    cores, halves, inner_count = (lax.axis_size(name) for name in ("core", "half", "inner"))
    core, half, inner = (lax.axis_index(name) for name in ("core", "half", "inner"))
    row_count = cores * inner_count
    my_index = core * inner_count + inner
    col_width = CROP // row_count
    per_group = CH // row_count
    chunk = CROP // SPLIT
    held_ids = crop_tiles[0]
    other_ids = lax.ppermute(held_ids, "core", [(0, 1), (1, 0)])
    crop_ids = jnp.where(core == half, held_ids, other_ids)
    position = crop_ids[:, None] * TILE + jnp.arange(TILE, dtype=jnp.int32)
    usable = (position < full_length[0]).astype(jnp.float32).reshape(CROP)
    col_usable = lax.dynamic_slice_in_dim(usable, my_index * col_width, col_width)
    pair_mask = col_usable[:, None] * usable[None, :]
    send = pack(held_ids, jnp.transpose(pair_maps[0], (0, 2, 1)))
    send = send.reshape(CH, row_count, col_width, TILE)
    wides, outs, final_wide = widen(proj_weight, out_weight, final_weight)
    gots, gates, boths = [], [], []
    for part in range(COLUMN_PARTS):
        got = spread(send, part)
        gate, *sends = first_stage(part, True, crop_ids, got, wides, pair_mask)
        send = after(send, sends[0])
        gots.append(got)
        gates.append(gate)
        arrays = []
        for value in sends:
            arrays.append(exchange(value))
        boths.append(arrays)
    following = []
    for number in range(SPLIT):
        merged = exchange(depth_products(number, boths, chunk)).reshape(CH, col_width, chunk)
        following.append(
            middle_stage(0, number, crop_ids, gots, merged, gates, outs, wides, pair_mask)
        )
    rights = []
    for item in following:
        rights.append(exchange(item[1].reshape(row_count, per_group, col_width, chunk)))
    ready, arrived = [], []
    back = None
    for pair, _, gate, *lefts in following:
        for piece, left in enumerate(lefts):
            left = left.reshape(row_count, per_group, col_width, chunk // LEFT_PARTS)
            left = exchange(left if back is None else after(left, back))
            products = row_products(left, rights)
            back = exchange(products)
            merged = back.reshape(CH, col_width, chunk // LEFT_PARTS)
            ready.append(last_stage(NLAYER - 1, piece, pair, merged, gate, outs))
            arrived.append(moved(ready[-1], [((0, 1), (0, 0)), ((1, 0), (1, 1))]))
    hiddens, shareds = [], []
    for normed_final, across in zip(ready, arrived):
        summed = normed_final.astype(jnp.float32) + across.astype(jnp.float32)
        hiddens.append(jnp.maximum(summed / halves, 0.0).astype(jnp.bfloat16))
        shareds.append(moved(hiddens[-1], [((0, 0), (1, 0)), ((1, 1), (0, 1))]))
    home = (core == half).astype(jnp.int32)[None]
    result = None
    for number, (hidden, shared) in enumerate(zip(hiddens, shareds)):
        result = end_stage(home, number, len(hiddens), hidden, shared, final_wide, result)
    return result


def on_device(pair_maps, crop_tiles, full_length, proj_weight, out_weight, final_weight):
    row_count = lax.axis_size("row")
    my_index = lax.axis_index("row")
    pair_local = pair_maps[0]
    crop_ids = crop_tiles[0]
    local_rows = pair_local.shape[0]
    col_width = CROP // row_count
    parts_count = max(1, row_count // CH)
    per_group = CH * parts_count // row_count
    groups = CH // per_group
    part_rows = CROP // parts_count
    steps_crop = jnp.arange(CROP, dtype=jnp.int32)
    position = crop_ids[steps_crop // TILE] * TILE + steps_crop % TILE
    usable = (position < full_length[0]).astype(jnp.float32)
    col_usable = lax.dynamic_slice_in_dim(usable, my_index * col_width, col_width)
    pair_mask = col_usable[:, None] * usable[None, :]
    columns = pair_local.reshape(local_rows, FULL // TILE, TILE, CH)[:, crop_ids]
    columns = columns.reshape(local_rows, CROP * CH)
    received = lax.all_to_all(columns, "row", split_axis=1, concat_axis=0, tiled=True)
    cropped = received.reshape(FULL // TILE, TILE, col_width * CH)[crop_ids]
    current = jnp.transpose(cropped.reshape(CROP, col_width, CH), (2, 1, 0))
    for layer_idx in range(NLAYER):
        normed_in = channel_norm(current.astype(jnp.float32)).astype(jnp.bfloat16)
        projected = jnp.einsum(
            "cd,cwi->dwi", proj_weight[layer_idx], normed_in, preferred_element_type=jnp.float32
        )
        left_proj = (jax.nn.sigmoid(projected[:CH]) * projected[CH : 2 * CH] * pair_mask).astype(
            jnp.bfloat16
        )
        right_proj = (
            jax.nn.sigmoid(projected[2 * CH : 3 * CH]) * projected[3 * CH : 4 * CH] * pair_mask
        ).astype(jnp.bfloat16)
        gate_vals = jax.nn.sigmoid(projected[4 * CH :])
        left_send = left_proj.reshape(groups, per_group, col_width, parts_count, part_rows)
        left_send = jnp.transpose(left_send, (0, 3, 1, 2, 4)).reshape(
            row_count, per_group, col_width, part_rows
        )
        right_send = right_proj.reshape(groups, per_group, col_width, parts_count, part_rows)
        right_send = jnp.transpose(right_send, (0, 3, 1, 2, 4)).reshape(
            row_count, per_group, col_width, part_rows
        )
        left_got, right_got = (
            lax.all_to_all(left_send, "row", split_axis=0, concat_axis=2, tiled=True),
            lax.all_to_all(right_send, "row", split_axis=0, concat_axis=2, tiled=True),
        )
        right_whole = right_got[0]
        for bit_pos in range(parts_count.bit_length() - 1):
            partner = from_partner(right_whole, "row", bit_pos)
            lower_side = my_index // (1 << bit_pos) % 2 == 0
            right_whole = jnp.where(
                lower_side,
                jnp.concatenate([right_whole, partner], axis=2),
                jnp.concatenate([partner, right_whole], axis=2),
            )
        products = jnp.einsum(
            "cki,ckj->cij", left_got[0], right_whole, preferred_element_type=jnp.float32
        ).astype(jnp.bfloat16)
        back_send = jnp.transpose(
            products.reshape(per_group, part_rows, row_count, col_width), (2, 0, 3, 1)
        )
        back_got = lax.all_to_all(back_send, "row", split_axis=0, concat_axis=0, tiled=True)
        merged = back_got.reshape(groups, parts_count, per_group, col_width, part_rows)
        merged = jnp.transpose(merged, (0, 2, 3, 1, 4)).reshape(CH, col_width, CROP)
        normed_out = channel_norm(merged.astype(jnp.float32)).astype(jnp.bfloat16)
        update = jnp.einsum(
            "cd,cwi->dwi", out_weight[layer_idx], normed_out, preferred_element_type=jnp.float32
        )
        current = (current.astype(jnp.float32) + gate_vals * update).astype(jnp.bfloat16)
    normed_final = channel_norm(current.astype(jnp.float32))
    template_count = lax.axis_size("tmpl")
    summed = lax.psum(normed_final.astype(jnp.bfloat16), "tmpl").astype(jnp.float32)
    hidden = jnp.maximum(summed / template_count, 0.0).astype(jnp.bfloat16)
    result = jnp.einsum(
        "cz,cwi->zwi", final_weight, hidden, preferred_element_type=jnp.float32
    ).astype(jnp.bfloat16)
    return result


def solution(mesh):
    rows, templates = mesh.shape["row"], mesh.shape["tmpl"]
    whole_tiles = FULL // rows == TILE and CH % rows == 0
    if whole_tiles and templates == 2:
        grid = Mesh(
            mesh.devices.reshape(templates, templates, rows // templates),
            ("core", "half", "inner"),
        )
        lines = ("half", "inner")
        placed = (P("core", lines, None, None), P("core", None), P(), P(), P(), P())
        return jax.shard_map(
            in_halves, mesh=grid, in_specs=placed, out_specs=P(None, lines, None), check_vma=False
        )
    placed = (P("tmpl", "row", None, None), P("tmpl", None), P(), P(), P(), P())
    return jax.shard_map(
        on_device, mesh=mesh, in_specs=placed, out_specs=P(None, "row", None), check_vma=False
    )
```

```python
import functools

import jax
import jax.numpy as jnp
from jax import lax
from jax.experimental import pallas as pl
from jax.experimental.pallas import tpu as pltpu
from jax.sharding import Mesh, PartitionSpec as P

CH = 64
CROP = 1024
TILE = 128
NLAYER = 2
FULL = 2048


EPSILON = 1e-05


def from_partner(value, axis, bit):
    mask = 2**bit
    pairs = [(source, source ^ mask) for source in range(lax.axis_size(axis))]
    return lax.ppermute(value, axis, pairs)


def channel_norm(values):
    center = values - jnp.mean(values, axis=0, keepdims=True)
    spread = jnp.mean(center * center, axis=0, keepdims=True)
    return center * lax.rsqrt(spread + EPSILON)


SPLIT = 2
SUB = 8
PARTS = 2
COLUMN_PARTS = 2
LEFT_PARTS = (1, 2)


def widened(weight, source):
    depth, columns = weight.shape
    size = source.shape[0]
    pick = (source == lax.broadcasted_iota(jnp.int32, (size, columns), 1)).astype(weight.dtype)
    taken = lax.dot_general(
        pick, weight, (((1,), (1,)), ((), ())), preferred_element_type=jnp.float32
    ).astype(weight.dtype)
    grow = lax.broadcasted_iota(jnp.int32, (depth, depth * SUB), 1) // SUB
    grow = (grow == lax.broadcasted_iota(jnp.int32, grow.shape, 0)).astype(weight.dtype)
    wide = jnp.dot(taken, grow, preferred_element_type=jnp.float32)
    row = lax.broadcasted_iota(jnp.int32, wide.shape, 0) % SUB
    lane = lax.broadcasted_iota(jnp.int32, wide.shape, 1) % SUB
    return jnp.where(row == lane, wide, 0.0).astype(weight.dtype)


def widen_kernel(proj_ref, out_ref, final_ref, wide_ref, out_wide_ref, final_wide_ref):
    size = CH // PARTS

    @pl.loop(0, NLAYER)
    def _(layer):
        for part in range(PARTS):
            rows = lax.broadcasted_iota(jnp.int32, (5 * size * SUB, 5 * CH), 0) // SUB
            source = rows // size * CH + part * size + rows % size
            wide_ref[layer, part] = widened(proj_ref[layer], source)
        rows = lax.broadcasted_iota(jnp.int32, (CH * SUB, CH), 0) // SUB
        out_wide_ref[layer] = widened(out_ref[layer], rows)

    columns = final_ref.shape[1]
    rows = lax.broadcasted_iota(jnp.int32, (columns * SUB, columns), 0) // SUB
    final_wide_ref[...] = widened(final_ref[...], rows)


def widen(proj_weight, out_weight, final_weight):
    kind = proj_weight.dtype
    return pl.pallas_call(
        widen_kernel,
        out_shape=[
            jax.ShapeDtypeStruct((NLAYER, PARTS, 5 * CH // PARTS * SUB, CH * SUB), kind),
            jax.ShapeDtypeStruct((NLAYER, CH * SUB, CH * SUB), kind),
            jax.ShapeDtypeStruct((final_weight.shape[1] * SUB, CH * SUB), kind),
        ],
        compiler_params=PARAMS,
    )(proj_weight, out_weight, final_weight)


def sigmoid(values):
    return 0.5 * jnp.tanh(0.5 * values) + 0.5


def flat_dot(weight, values):
    channels, sub, lanes = values.shape
    return jnp.dot(
        weight,
        values.reshape(channels * sub, lanes).astype(jnp.bfloat16),
        preferred_element_type=jnp.float32,
    ).reshape(weight.shape[0] // sub, sub, lanes)


def project(values, wide_ref, mask_ref, store):
    normed = channel_norm(values)
    mask = mask_ref[...][None]
    size = CH // PARTS
    for part in range(PARTS):
        projected = flat_dot(wide_ref[part], normed)
        left = sigmoid(projected[:size]) * projected[size : 2 * size] * mask
        right = sigmoid(projected[2 * size : 3 * size]) * projected[3 * size : 4 * size] * mask
        gate = sigmoid(projected[4 * size :])
        pieces = [item.astype(jnp.bfloat16) for item in (left, right, gate)]
        store(slice(part * size, (part + 1) * size), *pieces)


def updated(values, back_ref, gate, out_ref):
    normed = channel_norm(back_ref[...].astype(jnp.float32))
    update = flat_dot(out_ref[...], normed)
    return (values + gate * update).astype(jnp.bfloat16)


def tiles_of(refs):
    return jnp.concatenate([ref[...].astype(jnp.float32) for ref in refs], axis=-1)


def first_kernel(per, ids_ref, *refs):
    wide_ref, mask_ref, gate_ref, *send_refs = refs[per:]
    group, sub, lanes = send_refs[0].shape[-3:]

    def store(piece, left, right, gate):
        place = slice(piece.start // group, piece.stop // group)
        for side, value in enumerate((left, right)):
            value = value.reshape(-1, group, sub, lanes)
            if len(send_refs) == 1:
                send_refs[0][place, side] = value
            else:
                send_refs[side][place] = value
        gate_ref[piece] = gate

    project(tiles_of(refs[:per]), wide_ref, mask_ref, store)


def middle_kernel(parts, per, count, ids_ref, *refs):
    tiles, refs = refs[: parts * per], refs[parts * per :]
    gates, refs = refs[:parts], refs[parts:]
    back_ref, out_ref, wide_ref, mask_ref, pair_ref, right_ref, next_ref = refs[:7]
    left_refs = refs[7:]

    def store(piece, left, right, gate):
        right_ref[piece] = right
        next_ref[piece] = gate
        for number, left_ref in enumerate(left_refs):
            lanes = left_ref.shape[-1]
            left_ref[piece] = left[:, :, number * lanes : (number + 1) * lanes]

    values = tiles_of(tiles[:per])
    gate = gates[0][...].astype(jnp.float32)
    for part in range(1, parts):
        reached = pl.program_id(0) >= part * count
        values = jnp.where(reached, tiles_of(tiles[part * per : (part + 1) * per]), values)
        gate = jnp.where(reached, gates[part][...].astype(jnp.float32), gate)
    pair = updated(values, back_ref, gate, out_ref)
    pair_ref[...] = pair
    project(pair.astype(jnp.float32), wide_ref, mask_ref, store)


def last_kernel(pair_ref, back_ref, gate_ref, out_ref, final_ref):
    gate = gate_ref[...].astype(jnp.float32)
    pair = updated(pair_ref[...].astype(jnp.float32), back_ref, gate, out_ref)
    final_ref[...] = channel_norm(pair.astype(jnp.float32)).astype(final_ref.dtype)


def end_kernel(home_ref, hidden_ref, shared_ref, wide_ref, *refs):
    hidden = jnp.where(
        home_ref[0] == 1, hidden_ref[...].astype(jnp.float32), shared_ref[...].astype(jnp.float32)
    )
    refs[-1][...] = flat_dot(wide_ref[...], hidden).astype(refs[-1].dtype)


PARAMS = pltpu.CompilerParams(vmem_limit_bytes=48 << 20)


def cost(flops, moved_bytes):
    return pl.CostEstimate(flops=int(flops), bytes_accessed=int(moved_bytes), transcendentals=0)


def by_columns(shape):
    return pl.BlockSpec((shape[0], SUB, shape[2]), lambda w, *_: (0, w, 0))


def whole(shape):
    return pl.BlockSpec(shape, lambda w, *_: (0,) * len(shape))


def layer_of(shape, layer):
    return pl.BlockSpec((None, *shape[1:]), lambda w, *_: (layer,) + (0,) * (len(shape) - 1))


def tile_specs(got, per, place):
    def at(tile):
        def index(*position):
            number, column = place(*position[:-1])
            return position[-1][number * per + tile], 0, column, 0

        return pl.BlockSpec((None, got.shape[1], SUB, got.shape[3]), index)

    return [at(tile) for tile in range(per)]


def part_column(part, count):
    return lambda w: jnp.clip(w - part * count, 0, count - 1)


def stage(kernel, specs, out_shapes, ids, operands, flops):
    moved_bytes = sum(2 * shape.size for shape in out_shapes) * 2
    width = out_shapes[0].shape[1]
    return pl.pallas_call(
        kernel,
        grid_spec=pltpu.PrefetchScalarGridSpec(
            num_scalar_prefetch=1,
            grid=(width // SUB,),
            in_specs=specs,
            out_specs=[by_columns(shape.shape) for shape in out_shapes],
        ),
        out_shape=out_shapes,
        compiler_params=PARAMS,
        cost_estimate=cost(flops, moved_bytes),
    )(ids, *operands)


def first_stage(part, joint, ids, got, wide, mask):
    targets, channels, width, tile = got.shape
    per = ids.shape[0] // SPLIT
    lanes = per * tile
    count = width // SUB
    group = channels // targets
    lead, copies = ((targets, 2), 1) if joint else ((targets,), 2)
    zeros = (0,) * (len(lead) + 1)
    specs = tile_specs(got, per, lambda n, w: (n, w)) + [
        pl.BlockSpec((None, *wide.shape[1:]), lambda n, w, _: (0, 0, 0, 0)),
        pl.BlockSpec((SUB, lanes), lambda n, w, _: (part * count + w, n)),
    ]
    return pl.pallas_call(
        functools.partial(first_kernel, per),
        grid_spec=pltpu.PrefetchScalarGridSpec(
            num_scalar_prefetch=1,
            grid=(SPLIT, count),
            in_specs=specs,
            out_specs=[pl.BlockSpec((channels, SUB, lanes), lambda n, w, _: (0, w, n))]
            + [pl.BlockSpec((*lead, group, SUB, lanes), lambda n, w, _: (*zeros, w, n))] * copies,
        ),
        out_shape=[jax.ShapeDtypeStruct((channels, width, SPLIT * lanes), got.dtype)]
        + [jax.ShapeDtypeStruct((*lead, group, width, SPLIT * lanes), got.dtype)] * copies,
        compiler_params=PARAMS,
        cost_estimate=cost(
            2 * wide.size // NLAYER * count * SPLIT * lanes, 8 * channels * width * SPLIT * lanes
        ),
    )(ids, *[got] * per, wide, mask)


def middle_stage(layer, number, ids, gots, back, gates, out_wide, wide, mask):
    _, channels, width, tile = gots[0].shape
    per = ids.shape[0] // SPLIT
    lanes = per * tile
    count = width // SUB
    shape = jax.ShapeDtypeStruct((channels, width * len(gots), lanes), back.dtype)
    specs, operands = [], []
    for part, got in enumerate(gots):
        column = part_column(part, count)
        specs += tile_specs(got, per, lambda w, column=column: (number, column(w)))
        operands += [got] * per
    for part, gate in enumerate(gates):
        column = part_column(part, count)
        specs.append(
            pl.BlockSpec(
                (channels, SUB, lanes), lambda w, _, column=column: (0, column(w), number)
            )
        )
        operands.append(gate)
    specs += [
        by_columns(back.shape),
        layer_of(out_wide.shape, layer),
        layer_of(wide.shape, layer + 1),
        pl.BlockSpec((SUB, lanes), lambda w, _: (w, number)),
    ]
    operands += [back, out_wide, wide, mask]
    kernel = functools.partial(middle_kernel, len(gots), per, count)
    flops = 2 * (wide.size + out_wide.size) // NLAYER * count * len(gots) * lanes
    pieces = LEFT_PARTS[number]
    left = jax.ShapeDtypeStruct((*shape.shape[:2], lanes // pieces), back.dtype)
    return stage(kernel, specs, [shape] * 3 + [left] * pieces, ids, operands, flops)


def last_stage(layer, piece, pair, back, gate, out_wide):
    block = pl.BlockSpec((back.shape[0], SUB, back.shape[2]), lambda w: (0, w, piece))
    return pl.pallas_call(
        last_kernel,
        grid=(back.shape[1] // SUB,),
        in_specs=[block, by_columns(back.shape), block, layer_of(out_wide.shape, layer)],
        out_specs=by_columns(back.shape),
        out_shape=jax.ShapeDtypeStruct(back.shape, back.dtype),
        compiler_params=PARAMS,
        cost_estimate=cost(out_wide.size * back.size // CH // SUB, 8 * back.size),
    )(pair, back, gate, out_wide)


def end_stage(home, start, total, hidden, shared, wide, earlier):
    width, lanes = hidden.shape[1:]
    columns = wide.shape[0] // SUB
    out = jax.ShapeDtypeStruct((columns, width, total), hidden.dtype)
    specs = [by_columns(hidden.shape)] * 2 + [whole(wide.shape)]
    operands = [hidden, shared, wide]
    if earlier is not None:
        specs.append(pl.BlockSpec(memory_space=pl.ANY))
        operands.append(earlier)
    return pl.pallas_call(
        end_kernel,
        grid_spec=pltpu.PrefetchScalarGridSpec(
            num_scalar_prefetch=1,
            grid=(width // SUB,),
            in_specs=specs,
            out_specs=pl.BlockSpec((columns, SUB, lanes), lambda w, _: (0, w, start // lanes)),
        ),
        out_shape=out,
        input_output_aliases={} if earlier is None else {4: 0},
        compiler_params=PARAMS,
        cost_estimate=cost(2 * wide.size * width // SUB * lanes, 8 * hidden.size),
    )(home, *operands)


def product_kernel(axis, count, *refs):
    lefts, rights, out_ref = refs[:count], refs[count:-1], refs[-1]
    targets, _, width, chunk = out_ref.shape

    def matrix(ref):
        value = ref[...]
        return value.reshape(value.shape[0] * value.shape[-2], value.shape[-1])

    def times(left, right):
        return lax.dot_general(
            right, left, (((0,), (0,)), ((), ())), preferred_element_type=jnp.float32
        )

    if axis == "depth":
        left = jnp.concatenate([matrix(ref) for ref in lefts], axis=0)
        right = jnp.concatenate([matrix(ref) for ref in rights], axis=0)
        pieces = [times(left, right)]
    else:
        pieces = [times(matrix(lefts[0]), matrix(right)) for right in rights]
    per = targets // len(pieces)
    for number, piece in enumerate(pieces):
        out_ref[number * per : (number + 1) * per] = piece.astype(out_ref.dtype).reshape(
            per, 1, width, chunk
        )


def product_call(axis, specs, operands, count, out):
    targets, channels, width, chunk = out.shape
    return pl.pallas_call(
        functools.partial(product_kernel, axis, count),
        grid=(channels,),
        in_specs=specs,
        out_specs=pl.BlockSpec((targets, 1, width, chunk), lambda c: (0, c, 0, 0)),
        out_shape=out,
        compiler_params=pltpu.CompilerParams(vmem_limit_bytes=40 << 20),
        cost_estimate=cost(2 * out.size * targets * width, 8 * out.size),
    )(*operands)


def depth_products(number, boths, chunk):
    targets, channels = boths[0][0].shape[0], boths[0][0].shape[-3]
    specs, operands, depth = [], [], 0
    for side in range(2):
        for arrays in boths:
            width, lanes = arrays[0].shape[-2:]
            size, place = (lanes, 0) if side else (chunk, number)
            if len(arrays) == 1:
                spec = pl.BlockSpec(
                    (targets, None, 1, width, size),
                    lambda c, side=side, place=place: (0, side, c, 0, place),
                )
            else:
                spec = pl.BlockSpec(
                    (targets, 1, width, size), lambda c, place=place: (0, c, 0, place)
                )
            specs.append(spec)
            operands.append(arrays[0] if len(arrays) == 1 else arrays[side])
            depth += (1 - side) * width
    out = jax.ShapeDtypeStruct((targets, channels, depth, chunk), operands[0].dtype)
    return product_call("depth", specs, operands, len(boths), out)


def row_products(left, rights):
    targets, _, width, _ = left.shape

    def spec(array):
        return pl.BlockSpec((targets, 1, width, array.shape[3]), lambda c: (0, c, 0, 0))

    out = jax.ShapeDtypeStruct(left.shape, left.dtype)
    specs = [spec(array) for array in (left, *rights)]
    return product_call("rows", specs, [left, *rights], 1, out)


def pack_kernel(ids_ref, rows_ref, packed_ref):
    rows = rows_ref[...].astype(jnp.float32)
    packed_ref[...] = jnp.swapaxes(jnp.swapaxes(rows, 0, 1), 1, 2).astype(packed_ref.dtype)


def pack(ids, rows):
    tile, channels, _ = rows.shape
    slots = ids.shape[0]
    group = 2 * SUB
    out = jax.ShapeDtypeStruct((channels, slots * TILE, tile), rows.dtype)
    return pl.pallas_call(
        pack_kernel,
        grid_spec=pltpu.PrefetchScalarGridSpec(
            num_scalar_prefetch=1,
            grid=(slots, channels // group),
            in_specs=[pl.BlockSpec((tile, group, TILE), lambda s, c, ids: (0, c, ids[s]))],
            out_specs=pl.BlockSpec((group, TILE, tile), lambda s, c, ids: (c, s, 0)),
        ),
        out_shape=out,
        compiler_params=PARAMS,
        cost_estimate=cost(0, 4 * out.size),
    )(ids, rows)


def spread_kernel(part, send_ref, got_ref, hold, send_sem, recv_sem, hold_sem):
    columns = pl.ds(part * got_ref.shape[2], got_ref.shape[2])
    core, half, inner = (lax.axis_index(name) for name in ("core", "half", "inner"))
    cores, halves, width = (lax.axis_size(name) for name in ("core", "half", "inner"))
    blocks = cores * width
    row = half * width + inner
    mine = core * width + inner
    barrier = pltpu.get_barrier_semaphore()
    total = cores * halves * width
    flat = (core * halves + half) * width + inner
    for step in range(1, total):
        other = lax.rem(flat + step, total)
        pl.semaphore_signal(
            barrier,
            inc=1,
            device_id={
                "core": other // (halves * width),
                "half": lax.rem(other // width, halves),
                "inner": lax.rem(other, width),
            },
            device_id_type=pl.DeviceIdType.MESH,
        )
    pl.semaphore_wait(barrier, total - 1)

    def outgoing(step):
        block = lax.rem(mine + step, blocks)
        return pltpu.make_async_remote_copy(
            src_ref=send_ref.at[:, block, columns],
            dst_ref=got_ref.at[row],
            send_sem=send_sem.at[step],
            recv_sem=recv_sem.at[row],
            device_id={"core": block // width, "half": core, "inner": lax.rem(block, width)},
            device_id_type=pl.DeviceIdType.MESH,
        )

    home = half == core
    for step in range(1, blocks):
        outgoing(step).start()

    @pl.when(home)
    def _():
        bring = pltpu.make_async_copy(send_ref.at[:, mine, columns], hold, hold_sem.at[0])
        bring.start()
        bring.wait()
        put = pltpu.make_async_copy(hold, got_ref.at[row], hold_sem.at[1])
        put.start()
        put.wait()

    @pl.when(jnp.logical_not(home))
    def _():
        outgoing(0).start()

    def incoming(slot):
        return pltpu.make_async_remote_copy(
            src_ref=send_ref.at[:, 0, columns],
            dst_ref=got_ref.at[slot],
            send_sem=send_sem.at[0],
            recv_sem=recv_sem.at[slot],
            device_id={"core": core, "half": half, "inner": inner},
            device_id_type=pl.DeviceIdType.MESH,
        )

    for step in range(1, blocks):
        outgoing(step).wait_send()

    @pl.when(jnp.logical_not(home))
    def _():
        outgoing(0).wait_send()

    for step in range(1, blocks):
        incoming(lax.rem(row + step, blocks)).wait_recv()

    @pl.when(jnp.logical_not(home))
    def _():
        incoming(row).wait_recv()


def spread(send, part):
    channels, blocks, width, tile = send.shape
    width = width // COLUMN_PARTS
    return pl.pallas_call(
        functools.partial(spread_kernel, part),
        in_specs=[pl.BlockSpec(memory_space=pl.ANY)],
        out_specs=pl.BlockSpec(memory_space=pl.ANY),
        out_shape=jax.ShapeDtypeStruct((blocks, channels, width, tile), send.dtype),
        scratch_shapes=[
            pltpu.VMEM((channels, width, tile), send.dtype),
            pltpu.SemaphoreType.DMA((blocks,)),
            pltpu.SemaphoreType.DMA((blocks,)),
            pltpu.SemaphoreType.DMA((2,)),
        ],
        compiler_params=pltpu.CompilerParams(
            collective_id=part, has_side_effects=True, vmem_limit_bytes=32 << 20
        ),
        cost_estimate=cost(0, 64 * blocks * channels * width * tile),
    )(send)


GROUP = ("core", "inner")


def exchange(value):
    return lax.all_to_all(value, GROUP, split_axis=0, concat_axis=0, tiled=True)


def moved(value, pairs):
    halves = lax.axis_size("half")
    steps = [(a * halves + b, c * halves + d) for (a, b), (c, d) in pairs]
    return lax.ppermute(value, ("core", "half"), steps)


def after(value, *others):
    return lax.optimization_barrier((value, *others))[0]


def in_halves(pair_maps, crop_tiles, full_length, proj_weight, out_weight, final_weight):
    cores, halves, inner_count = (lax.axis_size(name) for name in ("core", "half", "inner"))
    core, half, inner = (lax.axis_index(name) for name in ("core", "half", "inner"))
    row_count = cores * inner_count
    my_index = core * inner_count + inner
    col_width = CROP // row_count
    per_group = CH // row_count
    chunk = CROP // SPLIT
    held_ids = crop_tiles[0]
    other_ids = lax.ppermute(held_ids, "core", [(0, 1), (1, 0)])
    crop_ids = jnp.where(core == half, held_ids, other_ids)
    position = crop_ids[:, None] * TILE + jnp.arange(TILE, dtype=jnp.int32)
    usable = (position < full_length[0]).astype(jnp.float32).reshape(CROP)
    col_usable = lax.dynamic_slice_in_dim(usable, my_index * col_width, col_width)
    pair_mask = col_usable[:, None] * usable[None, :]
    send = pack(held_ids, jnp.transpose(pair_maps[0], (0, 2, 1)))
    send = send.reshape(CH, row_count, col_width, TILE)
    wides, outs, final_wide = widen(proj_weight, out_weight, final_weight)
    gots, gates, boths = [], [], []
    for part in range(COLUMN_PARTS):
        got = spread(send, part)
        gate, *sends = first_stage(part, True, crop_ids, got, wides, pair_mask)
        send = after(send, sends[0])
        gots.append(got)
        gates.append(gate)
        arrays = []
        for value in sends:
            arrays.append(exchange(value))
        boths.append(arrays)
    following = []
    for number in range(SPLIT):
        merged = exchange(depth_products(number, boths, chunk)).reshape(CH, col_width, chunk)
        following.append(
            middle_stage(0, number, crop_ids, gots, merged, gates, outs, wides, pair_mask)
        )
    rights = []
    for item in following:
        rights.append(exchange(item[1].reshape(row_count, per_group, col_width, chunk)))
    ready, arrived = [], []
    back = None
    for pair, _, gate, *lefts in following:
        for piece, left in enumerate(lefts):
            left = left.reshape(row_count, per_group, col_width, left.shape[2])
            left = exchange(left if back is None else after(left, back))
            products = row_products(left, rights)
            back = exchange(products)
            merged = back.reshape(CH, col_width, back.shape[3])
            ready.append(last_stage(NLAYER - 1, piece, pair, merged, gate, outs))
            arrived.append(moved(ready[-1], [((0, 1), (0, 0)), ((1, 0), (1, 1))]))
    hiddens, shareds = [], []
    for normed_final, across in zip(ready, arrived):
        summed = normed_final.astype(jnp.float32) + across.astype(jnp.float32)
        hiddens.append(jnp.maximum(summed / halves, 0.0).astype(jnp.bfloat16))
        shareds.append(moved(hiddens[-1], [((0, 0), (1, 0)), ((1, 1), (0, 1))]))
    home = (core == half).astype(jnp.int32)[None]
    result, start = None, 0
    for hidden, shared in zip(hiddens, shareds):
        result = end_stage(home, start, CROP, hidden, shared, final_wide, result)
        start += hidden.shape[2]
    return result


def on_device(pair_maps, crop_tiles, full_length, proj_weight, out_weight, final_weight):
    row_count = lax.axis_size("row")
    my_index = lax.axis_index("row")
    pair_local = pair_maps[0]
    crop_ids = crop_tiles[0]
    local_rows = pair_local.shape[0]
    col_width = CROP // row_count
    parts_count = max(1, row_count // CH)
    per_group = CH * parts_count // row_count
    groups = CH // per_group
    part_rows = CROP // parts_count
    steps_crop = jnp.arange(CROP, dtype=jnp.int32)
    position = crop_ids[steps_crop // TILE] * TILE + steps_crop % TILE
    usable = (position < full_length[0]).astype(jnp.float32)
    col_usable = lax.dynamic_slice_in_dim(usable, my_index * col_width, col_width)
    pair_mask = col_usable[:, None] * usable[None, :]
    columns = pair_local.reshape(local_rows, FULL // TILE, TILE, CH)[:, crop_ids]
    columns = columns.reshape(local_rows, CROP * CH)
    received = lax.all_to_all(columns, "row", split_axis=1, concat_axis=0, tiled=True)
    cropped = received.reshape(FULL // TILE, TILE, col_width * CH)[crop_ids]
    current = jnp.transpose(cropped.reshape(CROP, col_width, CH), (2, 1, 0))
    for layer_idx in range(NLAYER):
        normed_in = channel_norm(current.astype(jnp.float32)).astype(jnp.bfloat16)
        projected = jnp.einsum(
            "cd,cwi->dwi", proj_weight[layer_idx], normed_in, preferred_element_type=jnp.float32
        )
        left_proj = (jax.nn.sigmoid(projected[:CH]) * projected[CH : 2 * CH] * pair_mask).astype(
            jnp.bfloat16
        )
        right_proj = (
            jax.nn.sigmoid(projected[2 * CH : 3 * CH]) * projected[3 * CH : 4 * CH] * pair_mask
        ).astype(jnp.bfloat16)
        gate_vals = jax.nn.sigmoid(projected[4 * CH :])
        left_send = left_proj.reshape(groups, per_group, col_width, parts_count, part_rows)
        left_send = jnp.transpose(left_send, (0, 3, 1, 2, 4)).reshape(
            row_count, per_group, col_width, part_rows
        )
        right_send = right_proj.reshape(groups, per_group, col_width, parts_count, part_rows)
        right_send = jnp.transpose(right_send, (0, 3, 1, 2, 4)).reshape(
            row_count, per_group, col_width, part_rows
        )
        left_got, right_got = (
            lax.all_to_all(left_send, "row", split_axis=0, concat_axis=2, tiled=True),
            lax.all_to_all(right_send, "row", split_axis=0, concat_axis=2, tiled=True),
        )
        right_whole = right_got[0]
        for bit_pos in range(parts_count.bit_length() - 1):
            partner = from_partner(right_whole, "row", bit_pos)
            lower_side = my_index // (1 << bit_pos) % 2 == 0
            right_whole = jnp.where(
                lower_side,
                jnp.concatenate([right_whole, partner], axis=2),
                jnp.concatenate([partner, right_whole], axis=2),
            )
        products = jnp.einsum(
            "cki,ckj->cij", left_got[0], right_whole, preferred_element_type=jnp.float32
        ).astype(jnp.bfloat16)
        back_send = jnp.transpose(
            products.reshape(per_group, part_rows, row_count, col_width), (2, 0, 3, 1)
        )
        back_got = lax.all_to_all(back_send, "row", split_axis=0, concat_axis=0, tiled=True)
        merged = back_got.reshape(groups, parts_count, per_group, col_width, part_rows)
        merged = jnp.transpose(merged, (0, 2, 3, 1, 4)).reshape(CH, col_width, CROP)
        normed_out = channel_norm(merged.astype(jnp.float32)).astype(jnp.bfloat16)
        update = jnp.einsum(
            "cd,cwi->dwi", out_weight[layer_idx], normed_out, preferred_element_type=jnp.float32
        )
        current = (current.astype(jnp.float32) + gate_vals * update).astype(jnp.bfloat16)
    normed_final = channel_norm(current.astype(jnp.float32))
    template_count = lax.axis_size("tmpl")
    summed = lax.psum(normed_final.astype(jnp.bfloat16), "tmpl").astype(jnp.float32)
    hidden = jnp.maximum(summed / template_count, 0.0).astype(jnp.bfloat16)
    result = jnp.einsum(
        "cz,cwi->zwi", final_weight, hidden, preferred_element_type=jnp.float32
    ).astype(jnp.bfloat16)
    return result


def solution(mesh):
    rows, templates = mesh.shape["row"], mesh.shape["tmpl"]
    whole_tiles = FULL // rows == TILE and CH % rows == 0
    if whole_tiles and templates == 2:
        grid = Mesh(
            mesh.devices.reshape(templates, templates, rows // templates),
            ("core", "half", "inner"),
        )
        lines = ("half", "inner")
        placed = (P("core", lines, None, None), P("core", None), P(), P(), P(), P())
        return jax.shard_map(
            in_halves, mesh=grid, in_specs=placed, out_specs=P(None, lines, None), check_vma=False
        )
    placed = (P("tmpl", "row", None, None), P("tmpl", None), P(), P(), P(), P())
    return jax.shard_map(
        on_device, mesh=mesh, in_specs=placed, out_specs=P(None, "row", None), check_vma=False
    )
```
